512 devices in a mesh: lat: 32 (over x, z_lo), lon: 16 (over y, z_hi, core).
Axes of the slice: x: 4, y: 4, z: 16 (z_hi: 2, z_lo: 8; z = z_hi * 8 + z_lo), core: 2. Of those that a mesh axis runs over, the one named last changes fastest.
Arguments:
- state: float32 [4, 2, 768, 2048], P(None, None, 'lat', 'lon'), may hold values from -6 to 6
- zonal_shift: int32 [2, 768], P(None, 'lat'), may hold values from -1024 to 1024, as said below
- zonal_cells: int32 [2, 768, 2048], P(None, 'lat', 'lon'), may hold values from -2 to 2
- zonal_fraction: float32 [2, 768, 2048], P(None, 'lat', 'lon'), may hold values from 0 to 1
- merid_cells: int32 [2, 768, 2048], P(None, 'lat', 'lon'), may hold values from -1 to 1
- merid_fraction: float32 [2, 768, 2048], P(None, 'lat', 'lon'), may hold values from 0 to 1
- coupling: float32 [2, 768, 2048], P(None, 'lat', 'lon'), may hold values from 0.5 to 8
Outputs:
- advanced: float32 [4, 2, 768, 2048], P(None, None, 'lat', 'lon')
The draws below stay inside these ranges and needn't reach their ends.
Inputs may be any that keep to these rules, and one draw needn't show every extreme that they name: `zonal_shift`: one whole-cell zonal displacement for each level and latitude row; bounded more tightly near the equator than near the poles.
All inputs are finite; a program needn't handle non-finite values.
Results may differ from the reference program's by a relative error of at most 0.00002.
Values sent between devices are 32-bit elements; how exact they have to be, the bound alone decides.
No kernel may reach another device: no remote copies, remote signals or barrier semaphores. Data moves between devices by JAX's collectives and lax.ppermute only.
A program may use at most 128 MiB of HBM per device.

```python
import math
import jax
import jax.numpy as jnp
from jax import lax

FIELDS = 4
LEV = 2
SWEEPS = 4
NLAT = 768
NLON = 2048


def draw_zonal_shift(key, part):
    rowids = jnp.arange(NLAT, dtype=jnp.int32)
    pole = jnp.minimum(rowids, NLAT - 1 - rowids)
    half = NLAT // 2
    span = NLON // 2
    reach = jnp.maximum(half - 1 - pole, 0)
    limit = 4 + (span - 4) * reach // max(half - 1, 1)
    limit = jnp.minimum(limit, span).astype(jnp.int32)
    lower = jnp.broadcast_to(-limit[None, :], (LEV, NLAT))
    upper = jnp.broadcast_to(limit[None, :] + 1, (LEV, NLAT))
    value = jax.random.randint(key, (LEV, NLAT), lower, upper, dtype=jnp.int32)
    levels = jnp.arange(LEV, dtype=jnp.int32)[:, None]
    edge = jnp.where(levels % 2 == 0, span, -span).astype(jnp.int32)
    value = jnp.where((rowids == 0)[None, :], edge, value)
    return value.astype(jnp.int32)


def set_ends(values, key, smallest, top_value):
    longest = values.shape.index(max(values.shape))
    spots = []
    for shift in (0, 1):
        where = [jax.random.randint(jax.random.fold_in(key, axis), (), 0, length) for axis, length in enumerate(values.shape)]
        where[longest] = (where[longest] + shift) % values.shape[longest]
        spots.append(tuple(where))
    return values.at[spots[0]].set(smallest).at[spots[1]].set(top_value)


def block_levels(stream_key, extent, split, low, high):
    gain, own = 1.0, jax.random.fold_in(stream_key, 6)
    for dim, parts in split:
        heights = jnp.exp(jax.random.uniform(jax.random.fold_in(own, dim), (parts,), jnp.float32, low / len(split), high / len(split)))
        gain = gain * jnp.repeat(heights, extent[dim] // parts).reshape([-1 if axis == dim else 1 for axis in range(len(extent))])
    return gain


def scatter_about(rng, shape, spread, most, cuts=(), kind=jnp.bfloat16):
    result = spread * jax.random.normal(rng, shape, jnp.float32)
    if cuts:
        result = result * block_levels(rng, shape, cuts, -0.22, 0.18)
    return jnp.clip(result, -most, most).astype(kind)


def setup_inputs(seed: int = 0) -> dict:
    keys = jax.random.split(jax.random.key(seed), 8)
    return {
        "state": scatter_about(keys[0], (FIELDS, LEV, NLAT, NLON), 1.0, 6.0, ((2, 32), (3, 16)), jnp.float32),
        "zonal_shift": draw_zonal_shift(jax.random.fold_in(keys[7], 71), 0),
        "zonal_cells": set_ends(jax.random.randint(keys[2], (LEV, NLAT, NLON), -2, 3), jax.random.fold_in(keys[2], 1), -2, 2).astype(jnp.int32),
        "zonal_fraction": jnp.clip(1.0 * jax.random.uniform(keys[3], (LEV, NLAT, NLON), jnp.float32) ** block_levels(keys[3], (LEV, NLAT, NLON), ((1, 32), (2, 16)), -0.2, 0.2), 0.0, 1.0),
        "merid_cells": set_ends(jax.random.randint(keys[4], (LEV, NLAT, NLON), -1, 2), jax.random.fold_in(keys[4], 1), -1, 1).astype(jnp.int32),
        "merid_fraction": jnp.clip(1.0 * jax.random.uniform(keys[5], (LEV, NLAT, NLON), jnp.float32) ** block_levels(keys[5], (LEV, NLAT, NLON), ((1, 32), (2, 16)), -0.2, 0.2), 0.0, 1.0),
        "coupling": jnp.clip(jnp.exp(math.log(8.0) - 2.7725887 * jax.random.uniform(keys[6], (LEV, NLAT, NLON), jnp.float32) ** block_levels(keys[6], (LEV, NLAT, NLON), ((1, 32), (2, 16)), -0.2, 0.2)), 0.5, 8.0),
    }


def cubic_weights(frac):
    return (-frac * (frac - 1.0) * (frac - 2.0) / 6.0,
            (frac + 1.0) * (frac - 1.0) * (frac - 2.0) / 2.0,
            -(frac + 1.0) * frac * (frac - 2.0) / 2.0,
            (frac + 1.0) * frac * (frac - 1.0) / 6.0)


def reference(state, zonal_shift, zonal_cells, zonal_fraction, merid_cells, merid_fraction, coupling):
    columns = jnp.arange(NLON, dtype=jnp.int32)
    rowids = jnp.arange(NLAT, dtype=jnp.int32)
    zonal_base = (columns[None, None, :] - zonal_shift[:, :, None] - zonal_cells).astype(jnp.int32)
    merid_base = (rowids[None, :, None] + 3 - merid_cells).astype(jnp.int32)
    zonal_w = cubic_weights(zonal_fraction)
    merid_w = cubic_weights(merid_fraction)

    def advance(field):
        zonal = jnp.zeros(field.shape, jnp.float32)
        for k in range(4):
            index = jnp.mod(zonal_base + (k - 1), NLON).astype(jnp.int32)
            zonal = zonal + zonal_w[k] * jnp.take_along_axis(field, index, axis=2)
        padded = jnp.pad(zonal, ((0, 0), (3, 3), (0, 0)))
        source = jnp.zeros(field.shape, jnp.float32)
        for k in range(4):
            index = (merid_base + (k - 1)).astype(jnp.int32)
            source = source + merid_w[k] * jnp.take_along_axis(padded, index, axis=1)
        phi = source
        for sweep in range(SWEEPS):
            rimmed = jnp.pad(phi, ((0, 0), (1, 1), (0, 0)))
            beside = rimmed[:, :-2, :] + rimmed[:, 2:, :]
            beside = beside + jnp.roll(phi, 1, axis=2) + jnp.roll(phi, -1, axis=2)
            phi = (source + coupling * beside) / (1.0 + 4.0 * coupling)
        return phi

    return lax.map(advance, state)
```

```python
import jax
import jax.numpy as jnp
from jax import lax
from jax.experimental import pallas as pl
from jax.experimental.pallas import tpu as pltpu
from jax.sharding import PartitionSpec as P

SWEEPS = 4
F32 = jnp.float32
I32 = jnp.int32
SECTORS = 16
Z_PAIRS = [[4 * y + c, 4 * y + 2 + c] for y in range(4) for c in range(2)]
Y_RINGS = [[4 * y + k for y in range(4)] for k in range(4)]
CORE_SWAP = [(i, i ^ 1) for i in range(SECTORS)]


def lanes(shape):
    return lax.broadcasted_iota(I32, shape, len(shape) - 1)


def cubic_weights(frac):
    return (
        -frac * (frac - 1.0) * (frac - 2.0) / 6.0,
        (frac + 1.0) * (frac - 1.0) * (frac - 2.0) / 2.0,
        -(frac + 1.0) * frac * (frac - 2.0) / 2.0,
        (frac + 1.0) * frac * (frac - 1.0) / 6.0,
    )


def offset_weights(frac, cells, lowest, highest):
    w = cubic_weights(frac)
    result = []
    for offset in range(-1 - highest, 3 - lowest):
        total = jnp.zeros_like(frac)
        for k in range(4):
            c = k - 1 - offset
            if lowest <= c <= highest:
                total = jnp.where(cells == float(c), w[k], total)
        result.append(total)
    return result


def pack_kernel(state, zc, zf, mc, mf, cp, out):
    rows = state.shape[2]
    for f in range(4):
        for l in range(2):
            out[2 * f + l] = state[f, l]
    lane = lanes((rows, 128))
    plane = jnp.zeros((rows, 128), F32)
    for i, ref in enumerate((zc, zf, mc, mf, cp)):
        for l in range(2):
            a = 2 * i + l
            moved = pltpu.roll(ref[l].astype(F32), 8 * a + 4, 1)
            plane = jnp.where(lane // 8 == a, moved, plane)
    out[8] = plane


def zonal_kernel(g0, g1, shift, zc, zf, mc, mf, cp, zonal, coef, ea, eb):
    rows = zc.shape[1]
    me, band = lax.axis_index("lon"), lax.axis_index("lat")
    core = me & 1
    lane = lanes((rows, 128))
    left, right = (me + SECTORS - 1) & 15, (me + 1) & 15
    before = g1[left // 4, (left // 2) & 1, 8]
    behind = g1[right // 4, (right // 2) & 1, 8]

    def extended(ref, i, l):
        a = 2 * i + l
        own = pltpu.roll(ref[l].astype(F32), 4, 1)
        first = jnp.where(lane < 4, pltpu.roll(before, (128 - 8 * a) % 128, 1), own)
        second = jnp.where(lane < 4, own, pltpu.roll(behind, (128 - 8 * a) % 128, 1))
        return jnp.concatenate([first, second], axis=1)

    eye = lax.broadcasted_iota(I32, (rows, rows), 0) == lax.broadcasted_iota(I32, (rows, rows), 1)
    for l in range(2):
        line = jnp.broadcast_to(shift[l : l + 1, :].astype(F32), (rows, rows))
        moved = jnp.sum(jnp.where(eye, line, 0.0), axis=1, keepdims=True).astype(I32)
        begin = jnp.broadcast_to((-moved - 7) & 2047, (rows, 128))
        place = (begin & 127) + lane
        index, inside = place & 127, place < 128
        sector = (me + (begin >> 7)) & 15
        weights = offset_weights(extended(zf, 1, l), extended(zc, 0, l), -2, 2)
        for f in range(4):
            fl = 2 * f + l
            block = [jnp.zeros((rows, 128), F32) for _ in range(3)]
            for y in range(4):
                for z in range(2):
                    for g, ref in enumerate((g0, g1)):
                        s = 4 * y + 2 * z + (core ^ g)
                        value = ref[y, z, fl]
                        for k in range(3):
                            block[k] = jnp.where(sector == ((s - k) & 15), value, block[k])
            r = [jnp.take_along_axis(v, index, axis=1) for v in block]
            window = jnp.concatenate(
                [jnp.where(inside, r[0], r[1]), jnp.where(inside, r[1], r[2])], axis=1
            )
            total = weights[0] * window
            for d in range(1, 8):
                total = total + weights[d] * pltpu.roll(window, 256 - d, 1)
            zonal[fl] = total
    for i, ref in enumerate((mc, mf, cp)):
        for l in range(2):
            coef[2 * i + l] = extended(ref, i + 2, l)
    even = (band & 1) == 0
    for out, base in ((ea, jnp.where(even, rows - 8, 0)), (eb, jnp.where(even, 0, rows - 8))):
        take = pl.ds(pl.multiple_of(base, 8), 8)
        lane8 = lanes((8, 128))
        plane = jnp.zeros((8, 128), F32)
        for fl in range(8):
            out[fl] = zonal[fl, take, 0:128]
            plane = jnp.where(lane8 // 8 == fl, pltpu.roll(zonal[fl, take, 128:256], 8 * fl, 1), plane)
        for a in range(6):
            out[9 + a] = coef[a, take, 0:128]
            plane = jnp.where(
                lane8 // 8 == 8 + a, pltpu.roll(coef[a, take, 128:256], 64 + 8 * a, 1), plane
            )
        out[8] = plane


def sweep_kernel(zonal, coef, ga, gb, out):
    rows = zonal.shape[1]
    total = rows + 16
    band, bands = lax.axis_index("lat"), lax.axis_size("lat")
    even = (band & 1) == 0

    def pick(plane):
        above = jnp.where(even, gb[0, plane], ga[0, plane])
        below = jnp.where(even, ga[1, plane], gb[1, plane])
        return above, below

    tails = pick(8)

    def joined(first, slot, own):
        ends = [
            jnp.concatenate([v, pltpu.roll(t, (128 - 8 * slot) % 128, 1)], axis=1)
            for v, t in zip(pick(first), tails)
        ]
        return jnp.concatenate([ends[0], own, ends[1]], axis=0)

    row = lax.broadcasted_iota(I32, (total, 256), 0)
    outside = ((row < 8) & (band == 0)) | ((row >= rows + 8) & (band == bands - 1))
    for l in range(2):
        cells = joined(9 + l, 8 + l, coef[l])
        frac = joined(11 + l, 10 + l, coef[2 + l])
        weights = offset_weights(frac, cells, -1, 1)
        coupling = joined(13 + l, 12 + l, coef[4 + l])
        inverse = jnp.where(outside, 0.0, 1.0 / (1.0 + 4.0 * coupling))
        factor = coupling * inverse
        for f in range(4):
            fl = 2 * f + l
            value = jnp.where(outside, 0.0, joined(fl, fl, zonal[fl]))
            source = jnp.zeros((total, 256), F32)
            for i, offset in enumerate(range(-2, 4)):
                moved = pltpu.roll(value, (-offset) % total, 0) if offset else value
                source = source + weights[i] * moved
            phi = jnp.where(outside, 0.0, source)
            source = source * inverse
            for _ in range(SWEEPS):
                beside = pltpu.roll(phi, 1, 0) + pltpu.roll(phi, total - 1, 0)
                beside = beside + pltpu.roll(phi, 1, 1) + pltpu.roll(phi, 255, 1)
                phi = source + factor * beside
            out[f, l] = pltpu.roll(phi[8 : 8 + rows], 252, 1)[:, 0:128]


def call(kernel, shapes):
    return pl.pallas_call(
        kernel,
        out_shape=[jax.ShapeDtypeStruct(s, F32) for s in shapes],
        compiler_params=pltpu.CompilerParams(vmem_limit_bytes=48 << 20),
    )


def body(state, zonal_shift, zonal_cells, zonal_fraction, merid_cells, merid_fraction, coupling):
    rows = state.shape[2]
    bands = lax.axis_size("lat")
    coefs = (zonal_cells, zonal_fraction, merid_cells, merid_fraction, coupling)

    def pairs(first):
        return [
            [(b % bands) * SECTORS + s for b in (i, i + 1)]
            for i in range(first, first + bands, 2)
            for s in range(SECTORS)
        ]

    (packed,) = call(pack_kernel, [(9, rows, 128)])(state, *coefs)
    both = lax.all_gather(packed, "lon", axis_index_groups=Z_PAIRS)
    own = lax.all_gather(both, "lon", axis_index_groups=Y_RINGS)
    other = lax.ppermute(own, "lon", CORE_SWAP)
    zonal, coef, ea, eb = call(
        zonal_kernel, [(8, rows, 256), (6, rows, 256), (15, 8, 128), (15, 8, 128)]
    )(own, other, zonal_shift, *coefs)
    ga = lax.all_gather(ea, ("lat", "lon"), axis_index_groups=pairs(0))
    gb = lax.all_gather(eb, ("lat", "lon"), axis_index_groups=pairs(1))
    (advanced,) = call(sweep_kernel, [state.shape])(zonal, coef, ga, gb)
    return advanced


def solution(mesh):
    in_specs = (
        P(None, None, "lat", "lon"),
        P(None, "lat"),
        P(None, "lat", "lon"),
        P(None, "lat", "lon"),
        P(None, "lat", "lon"),
        P(None, "lat", "lon"),
        P(None, "lat", "lon"),
    )
    out_specs = P(None, None, "lat", "lon")
    return jax.shard_map(body, mesh=mesh, in_specs=in_specs, out_specs=out_specs, check_vma=False)
```

```python
import jax
import jax.numpy as jnp
from jax import lax
from jax.experimental import pallas as pl
from jax.experimental.pallas import tpu as pltpu
from jax.sharding import PartitionSpec as P

SWEEPS = 4
F32 = jnp.float32
I32 = jnp.int32
SECTORS = 16
RUN = 8
Z_PAIRS = [[4 * y + c, 4 * y + 2 + c] for y in range(4) for c in range(2)]
Y_RINGS = [[4 * y + k for y in range(4)] for k in range(4)]
CORES = [[2 * i, 2 * i + 1] for i in range(SECTORS // 2)]


def iota(shape, dim):
    return lax.broadcasted_iota(I32, shape, dim)


def cubic_weights(frac):
    return (
        -frac * (frac - 1.0) * (frac - 2.0) / 6.0,
        (frac + 1.0) * (frac - 1.0) * (frac - 2.0) / 2.0,
        -(frac + 1.0) * frac * (frac - 2.0) / 2.0,
        (frac + 1.0) * frac * (frac - 1.0) / 6.0,
    )


def offset_weights(frac, cells, lowest, highest):
    w = cubic_weights(frac)
    result = []
    for offset in range(-1 - highest, 3 - lowest):
        total = jnp.zeros_like(frac)
        for k in range(4):
            c = k - 1 - offset
            if lowest <= c <= highest:
                total = jnp.where(cells == float(c), w[k], total)
        result.append(total)
    return result


def pack_rows(first, second, top):
    a = jnp.where(top, first, pltpu.roll(first, 4, 0))
    b = jnp.where(top, pltpu.roll(second, 4, 0), second)
    return jnp.where(iota((8, 128), 0) < 4, a, b)


def unpack_rows(packed):
    low = iota((8, 128), 0) < 4
    turned = pltpu.roll(packed, 4, 0)
    return jnp.where(low, packed, turned), jnp.where(low, turned, packed)


def place():
    me, band = lax.axis_index("lon"), lax.axis_index("lat")
    return me, band, (band & (RUN - 1)) == 0, (band & (RUN - 1)) == RUN - 1


def pack_kernel(*refs):
    sources, out, held, sems = refs[:6], refs[6], refs[7:13], refs[13]
    copies = [pltpu.make_async_copy(s, h, sems.at[i]) for i, (s, h) in enumerate(zip(sources, held))]
    for copy in copies:
        copy.start()
    for copy in copies:
        copy.wait()
    state, coefs = held[0], held[1:]
    rows = state.shape[2]
    for f in range(4):
        for l in range(2):
            at = (2 * f + l) * rows
            out[at : at + rows] = state[f, l]
    group = iota((rows, 128), 1) // 8
    plane = jnp.zeros((rows, 128), F32)
    for i, ref in enumerate(coefs):
        for l in range(2):
            a = 2 * i + l
            plane = jnp.where(group == a, pltpu.roll(ref[l].astype(F32), 8 * a + 4, 1), plane)
    out[8 * rows : 9 * rows] = plane
    _, _, opens, _ = place()

    def edge(ref, l):
        return jnp.where(opens, ref[l, 0:8], ref[l, rows - 8 : rows]).astype(F32)

    at = 9 * rows
    for ref in coefs[:2]:
        for l in range(2):
            out[at : at + 8] = edge(ref, l)
            at += 8
    for ref in coefs[2:]:
        out[at : at + 8] = pack_rows(edge(ref, 0), edge(ref, 1), opens)
        at += 8


def window_kernel(circle, shift, keep, send):
    rows = circle.shape[3]
    all_rows = rows + 8
    me, _, opens, _ = place()
    core = me & 1
    lane = iota((all_rows, 128), 1)
    flip = jnp.where(iota((all_rows, 128), 0) < rows, 0, 2)
    eye = iota((rows, rows), 0) == iota((rows, rows), 1)
    base = pl.multiple_of(jnp.where(opens, 0, rows - 8), 8)

    def block_of(y, z, plane):
        return jnp.concatenate([circle[y, z, plane], circle[y, z, plane, pl.ds(base, 8)]], axis=0)

    outs = (keep, send)
    slot = lane // 16
    tails = [jnp.zeros((all_rows, 128), F32) for _ in outs]
    for l in range(2):
        line = jnp.broadcast_to(shift[l : l + 1, :].astype(F32), (rows, rows))
        moved = jnp.sum(jnp.where(eye, line, 0.0), axis=1, keepdims=True).astype(I32)
        begin = jnp.broadcast_to((-moved - 7) & 2047, (rows, 128))
        begin = jnp.concatenate(
            [begin, jnp.where(opens, begin[0:8], begin[rows - 8 : rows])], axis=0
        )
        spot = (begin & 127) + lane
        index, inside = spot & 127, spot < 128
        hops = begin >> 7
        sectors = [((me ^ t ^ flip) + hops) & 15 for t in range(2)]
        for f in range(4):
            fl = 2 * f + l
            block = [[jnp.zeros((all_rows, 128), F32) for _ in range(3)] for _ in range(2)]
            for y in range(4):
                for z in range(2):
                    s = 4 * y + 2 * z + core
                    value = block_of(y, z, fl)
                    for t in range(2):
                        for k in range(3):
                            hit = sectors[t] == ((s - k) & 15)
                            block[t][k] = jnp.where(hit, value, block[t][k])
            for t, out in enumerate(outs):
                r = [jnp.take_along_axis(v, index, axis=1) for v in block[t]]
                out[fl] = jnp.where(inside, r[0], r[1])
                tail = pltpu.roll(jnp.where(inside, r[1], r[2]), 16 * fl, 1)
                tails[t] = jnp.where(slot == fl, tail, tails[t])
    for t, out in enumerate(outs):
        out[8] = tails[t]
    sides = []
    for step in (-1, 1):
        near = (((me ^ 1) + step) & 15) // 2
        far = (((me ^ 3) + step) & 15) // 2
        sides.append(
            jnp.concatenate(
                [circle[near // 2, near & 1, 8], circle[far // 2, far & 1, 8, pl.ds(base, 8)]],
                axis=0,
            )
        )
    send[9] = jnp.where((lane & 7) < 4, sides[0], sides[1])


def zonal_kernel(keep, swapped, around, zc, zf, mc, mf, cp, zonal, coef, ea, eb, edge_zonal, edge_coef):
    rows = zc.shape[1]
    all_rows = rows + 8
    me, band, opens, closes = place()
    mate = 1 - (me & 1)
    across = 1 - ((me >> 1) & 1)
    lane = iota((all_rows, 128), 1)
    beside = swapped[mate, 9]

    def extended(ref, extra, i, l):
        a = 2 * i + l
        own = jnp.concatenate([ref[l].astype(F32), extra], axis=0)
        own = pltpu.roll(own, 4, 1)
        side = pltpu.roll(beside, (128 - 8 * a) % 128, 1) if a else beside
        return jnp.concatenate(
            [jnp.where(lane < 4, side, own), jnp.where(lane < 4, own, side)], axis=1
        )

    def extra(n):
        at = 9 * rows + 8 * n
        return around[across, at : at + 8]

    for l in range(2):
        weights = offset_weights(
            extended(zf, extra(2 + l), 1, l), extended(zc, extra(l), 0, l), -2, 2
        )
        tails = keep[8] + swapped[mate, 8]
        for f in range(4):
            fl = 2 * f + l
            tail = pltpu.roll(tails, 128 - 16 * fl, 1) if fl else tails
            window = jnp.concatenate([keep[fl] + swapped[mate, fl], tail], axis=1)
            total = weights[0] * window
            for d in range(1, 8):
                total = total + weights[d] * pltpu.roll(window, 256 - d, 1)
            zonal[fl] = total[:rows]
            edge_zonal[fl] = total[rows:]
    for i, ref in enumerate((mc, mf, cp)):
        extras = unpack_rows(extra(4 + i))
        for l in range(2):
            wide = extended(ref, extras[l], i + 2, l)
            coef[2 * i + l] = wide[:rows]
            edge_coef[2 * i + l] = wide[rows:]

    even = (band & 1) == 0
    group = iota((8, 128), 1) // 8
    for out, top in ((ea, jnp.logical_not(even)), (eb, even)):
        take = pl.ds(pl.multiple_of(jnp.where(top, 0, rows - 8), 8), 8)
        at_end = opens | closes if out is eb else None

        def tile(ref, edge_ref, n):
            v = ref[n, take]
            return v if at_end is None else jnp.where(at_end, edge_ref[n], v)

        plane = jnp.zeros((8, 128), F32)
        for fl in range(8):
            v = tile(zonal, edge_zonal, fl)
            out[fl] = v[:, 0:128]
            tail = pltpu.roll(v[:, 128:256], 8 * fl, 1) if fl else v[:, 128:256]
            plane = jnp.where(group == fl, tail, plane)
        for i in range(3):
            pair = [tile(coef, edge_coef, 2 * i + l) for l in range(2)]
            out[9 + i] = pack_rows(pair[0][:, 0:128], pair[1][:, 0:128], top)
            for l in range(2):
                a = 8 + 2 * i + l
                plane = jnp.where(group == a, pltpu.roll(pair[l][:, 128:256], 8 * a, 1), plane)
        out[8] = plane


def sweep_kernel(zonal, coef, ga, gb, out):
    rows = zonal.shape[1]
    total = rows + 16
    band, bands = lax.axis_index("lat"), lax.axis_size("lat")
    even = (band & 1) == 0

    def pick(plane):
        above = jnp.where(even, gb[0, plane], ga[0, plane])
        below = jnp.where(even, ga[1, plane], gb[1, plane])
        return above, below

    tails = pick(8)

    def joined(firsts, slot, own):
        ends = [
            jnp.concatenate([v, pltpu.roll(t, 128 - 8 * slot, 1) if slot else t], axis=1)
            for v, t in zip(firsts, tails)
        ]
        return jnp.concatenate([ends[0], own, ends[1]], axis=0)

    row = iota((total, 256), 0)
    outside = ((row < 8) & (band == 0)) | ((row >= rows + 8) & (band == bands - 1))
    packs = [[unpack_rows(v) for v in pick(9 + i)] for i in range(3)]
    for l in range(2):
        cells, frac, coupling = [
            joined([v[l] for v in packs[i]], 8 + 2 * i + l, coef[2 * i + l]) for i in range(3)
        ]
        weights = offset_weights(frac, cells, -1, 1)
        inverse = jnp.where(outside, 0.0, 1.0 / (1.0 + 4.0 * coupling))
        factor = coupling * inverse
        for f in range(4):
            fl = 2 * f + l
            value = jnp.where(outside, 0.0, joined(pick(fl), fl, zonal[fl]))
            source = jnp.zeros((total, 256), F32)
            for i, offset in enumerate(range(-2, 4)):
                moved = pltpu.roll(value, (-offset) % total, 0) if offset else value
                source = source + weights[i] * moved
            phi = jnp.where(outside, 0.0, source)
            source = source * inverse
            for _ in range(SWEEPS):
                beside = pltpu.roll(phi, 1, 0) + pltpu.roll(phi, total - 1, 0)
                beside = beside + pltpu.roll(phi, 1, 1) + pltpu.roll(phi, 255, 1)
                phi = source + factor * beside
            out[f, l] = pltpu.roll(phi[8 : 8 + rows], 252, 1)[:, 0:128]


def call(kernel, shapes, scratch=(), in_specs=None):
    more = {} if in_specs is None else {"in_specs": in_specs}
    return pl.pallas_call(
        kernel,
        out_shape=[jax.ShapeDtypeStruct(s, F32) for s in shapes],
        scratch_shapes=list(scratch),
        compiler_params=pltpu.CompilerParams(vmem_limit_bytes=32 << 20),
        **more,
    )


def body(state, zonal_shift, zonal_cells, zonal_fraction, merid_cells, merid_fraction, coupling):
    rows = state.shape[2]
    bands = lax.axis_size("lat")
    coefs = (zonal_cells, zonal_fraction, merid_cells, merid_fraction, coupling)

    def pairs(first):
        return [
            [i * SECTORS + s, (i + 1) % bands * SECTORS + (s ^ 2 if i % RUN == RUN - 1 else s)]
            for i in range(first, first + bands, 2)
            for s in range(SECTORS)
        ]

    (packed,) = call(
        pack_kernel,
        [(9 * rows + 56, 128)],
        [pltpu.VMEM(v.shape, v.dtype) for v in (state, *coefs)] + [pltpu.SemaphoreType.DMA((6,))],
        [pl.BlockSpec(memory_space=pltpu.HBM)] * 6,
    )(state, *coefs)
    around = lax.all_gather(packed, "lon", axis_index_groups=Z_PAIRS)
    circle = lax.all_gather(around[:, : 9 * rows], "lon", axis_index_groups=Y_RINGS)
    keep, send = call(window_kernel, [(9, rows + 8, 128), (10, rows + 8, 128)])(
        circle.reshape(4, 2, 9, rows, 128), zonal_shift
    )
    swapped = lax.all_gather(send, "lon", axis_index_groups=CORES)
    zonal, coef, ea, eb = call(
        zonal_kernel,
        [(8, rows, 256), (6, rows, 256), (12, 8, 128), (12, 8, 128)],
        [pltpu.VMEM((8, 8, 256), F32), pltpu.VMEM((6, 8, 256), F32)],
    )(keep, swapped, around, *coefs)
    ga = lax.all_gather(ea, ("lat", "lon"), axis_index_groups=pairs(0))
    gb = lax.all_gather(eb, ("lat", "lon"), axis_index_groups=pairs(1))
    (advanced,) = call(sweep_kernel, [state.shape])(zonal, coef, ga, gb)
    return advanced


def solution(mesh):
    in_specs = (
        P(None, None, "lat", "lon"),
        P(None, "lat"),
        P(None, "lat", "lon"),
        P(None, "lat", "lon"),
        P(None, "lat", "lon"),
        P(None, "lat", "lon"),
        P(None, "lat", "lon"),
    )
    out_specs = P(None, None, "lat", "lon")
    return jax.shard_map(body, mesh=mesh, in_specs=in_specs, out_specs=out_specs, check_vma=False)
```

```python
import jax
import jax.numpy as jnp
from jax import lax
from jax.experimental import pallas as pl
from jax.experimental.pallas import tpu as pltpu
from jax.sharding import PartitionSpec as P

SWEEPS = 4
F32 = jnp.float32
I32 = jnp.int32
SECTORS = 16
Z_PAIRS = [[4 * y + c, 4 * y + 2 + c] for y in range(4) for c in range(2)]
Y_RINGS = [[4 * y + k for y in range(4)] for k in range(4)]
CORES = [[2 * i, 2 * i + 1] for i in range(SECTORS // 2)]


def iota(shape, dim):
    return lax.broadcasted_iota(I32, shape, dim)


def cubic_weights(frac):
    return (
        -frac * (frac - 1.0) * (frac - 2.0) / 6.0,
        (frac + 1.0) * (frac - 1.0) * (frac - 2.0) / 2.0,
        -(frac + 1.0) * frac * (frac - 2.0) / 2.0,
        (frac + 1.0) * frac * (frac - 1.0) / 6.0,
    )


def offset_weights(frac, cells, lowest, highest):
    w = cubic_weights(frac)
    result = []
    for offset in range(-1 - highest, 3 - lowest):
        total = jnp.zeros_like(frac)
        for k in range(4):
            c = k - 1 - offset
            if lowest <= c <= highest:
                total = jnp.where(cells == float(c), w[k], total)
        result.append(total)
    return result


def pack_rows(first, second, top):
    a = jnp.where(top, first, pltpu.roll(first, 4, 0))
    b = jnp.where(top, pltpu.roll(second, 4, 0), second)
    return jnp.where(iota((8, 128), 0) < 4, a, b)


def unpack_rows(packed):
    low = iota((8, 128), 0) < 4
    turned = pltpu.roll(packed, 4, 0)
    return jnp.where(low, packed, turned), jnp.where(low, turned, packed)


def pack_kernel(*refs):
    sources, out, begin, held, sems = refs[:7], refs[7], refs[8], refs[9:16], refs[16]
    copies = [pltpu.make_async_copy(s, h, sems.at[i]) for i, (s, h) in enumerate(zip(sources, held))]
    for copy in copies:
        copy.start()
    for copy in copies:
        copy.wait()
    state, shift, coefs = held[0], held[1], held[2:]
    rows = state.shape[2]
    group = iota((rows, 128), 1) // 8
    plane = jnp.zeros((rows, 128), F32)
    for i, ref in enumerate(coefs):
        for l in range(2):
            a = 2 * i + l
            plane = jnp.where(group == a, pltpu.roll(ref[l].astype(F32), 8 * a + 4, 1), plane)
    for peer in range(4):
        for f in range(4):
            for l in range(2):
                out[peer, 2 * f + l] = state[f, l]
        out[peer, 8] = plane
    eye = iota((rows, rows), 0) == iota((rows, rows), 1)
    for l in range(2):
        line = jnp.broadcast_to(shift[l : l + 1, :].astype(F32), (rows, rows))
        moved = jnp.sum(jnp.where(eye, line, 0.0), axis=1, keepdims=True).astype(I32)
        begin[l] = jnp.broadcast_to((-moved - 7) & 2047, (rows, 128))


def window_kernel(circle, begin, keep, send):
    rows = circle.shape[3]
    me = lax.axis_index("lon")
    core, side = me & 1, me & 2
    lane = iota((rows, 128), 1)
    outs = (keep, send)
    slot = lane // 16
    tails = [jnp.zeros((rows, 128), F32) for _ in outs]
    for l in range(2):
        spot = (begin[l] & 127) + lane
        index, inside = spot & 127, spot < 128
        hops = begin[l] >> 7
        sectors = [((me ^ (2 * t)) + hops) & 15 for t in range(2)]
        for f in range(4):
            fl = 2 * f + l
            block = [[jnp.zeros((rows, 128), F32) for _ in range(3)] for _ in range(2)]
            for y in range(4):
                for c in range(2):
                    s = 4 * y + side + c
                    value = circle[c, y, fl]
                    for t in range(2):
                        for k in range(3):
                            hit = sectors[t] == ((s - k) & 15)
                            block[t][k] = jnp.where(hit, value, block[t][k])
            for t, out in enumerate(outs):
                r = [jnp.take_along_axis(v, index, axis=1) for v in block[t]]
                out[fl] = jnp.where(inside, r[0], r[1])
                tail = jnp.where(inside, r[1], r[2])
                tail = pltpu.roll(tail, 16 * fl, 1) if fl else tail
                tails[t] = jnp.where(slot == fl, tail, tails[t])
    early = (lane & 7) < 4
    inner = circle[1 - core, (me // 4), 8]
    outer = ((me ^ 2) + jnp.where(core == 0, 15, 1)) & 15
    outer = circle[1 - core, outer // 4, 8]
    first = core == 0
    keep[9] = jnp.where(early != first, inner, 0.0)
    send[9] = jnp.where(early == first, outer, 0.0)
    for t, out in enumerate(outs):
        out[8] = tails[t]


def zonal_kernel(keep, swapped, zc, zf, mc, mf, cp, zonal, coef, ea, eb):
    rows = zc.shape[1]
    me, band = lax.axis_index("lon"), lax.axis_index("lat")
    across = 1 - ((me >> 1) & 1)
    lane = iota((rows, 128), 1)
    beside = keep[9] + swapped[across, 9]

    def extended(ref, i, l):
        a = 2 * i + l
        own = pltpu.roll(ref[l].astype(F32), 4, 1)
        side = pltpu.roll(beside, 128 - 8 * a, 1) if a else beside
        return jnp.concatenate(
            [jnp.where(lane < 4, side, own), jnp.where(lane < 4, own, side)], axis=1
        )

    tails = keep[8] + swapped[across, 8]
    for l in range(2):
        weights = offset_weights(extended(zf, 1, l), extended(zc, 0, l), -2, 2)
        for f in range(4):
            fl = 2 * f + l
            tail = pltpu.roll(tails, 128 - 16 * fl, 1) if fl else tails
            window = jnp.concatenate([keep[fl] + swapped[across, fl], tail], axis=1)
            total = weights[0] * window
            for d in range(1, 8):
                total = total + weights[d] * pltpu.roll(window, 256 - d, 1)
            zonal[fl] = total
    for i, ref in enumerate((mc, mf, cp)):
        for l in range(2):
            coef[2 * i + l] = extended(ref, i + 2, l)

    even = (band & 1) == 0
    group = iota((8, 128), 1) // 8
    for out, top in ((ea, jnp.logical_not(even)), (eb, even)):
        take = pl.ds(pl.multiple_of(jnp.where(top, 0, rows - 8), 8), 8)
        plane = jnp.zeros((8, 128), F32)
        for fl in range(8):
            v = zonal[fl, take]
            out[fl] = v[:, 0:128]
            tail = pltpu.roll(v[:, 128:256], 8 * fl, 1) if fl else v[:, 128:256]
            plane = jnp.where(group == fl, tail, plane)
        for i in range(3):
            pair = [coef[2 * i + l, take] for l in range(2)]
            out[9 + i] = pack_rows(pair[0][:, 0:128], pair[1][:, 0:128], top)
            for l in range(2):
                a = 8 + 2 * i + l
                plane = jnp.where(group == a, pltpu.roll(pair[l][:, 128:256], 8 * a, 1), plane)
        out[8] = plane


def sweep_kernel(zonal, coef, ga, gb, out):
    rows = zonal.shape[1]
    total = rows + 16
    band, bands = lax.axis_index("lat"), lax.axis_size("lat")
    even = (band & 1) == 0

    def pick(plane):
        above = jnp.where(even, gb[plane], ga[0, plane])
        below = jnp.where(even, ga[1, plane], gb[plane])
        return above, below

    tails = pick(8)

    def joined(firsts, slot, own):
        ends = [
            jnp.concatenate([v, pltpu.roll(t, 128 - 8 * slot, 1) if slot else t], axis=1)
            for v, t in zip(firsts, tails)
        ]
        return jnp.concatenate([ends[0], own, ends[1]], axis=0)

    row = iota((total, 256), 0)
    outside = ((row < 8) & (band == 0)) | ((row >= rows + 8) & (band == bands - 1))
    packs = [[unpack_rows(v) for v in pick(9 + i)] for i in range(3)]
    for l in range(2):
        cells, frac, coupling = [
            joined([v[l] for v in packs[i]], 8 + 2 * i + l, coef[2 * i + l]) for i in range(3)
        ]
        weights = offset_weights(frac, cells, -1, 1)
        inverse = jnp.where(outside, 0.0, 1.0 / (1.0 + 4.0 * coupling))
        factor = coupling * inverse
        for f in range(4):
            fl = 2 * f + l
            value = jnp.where(outside, 0.0, joined(pick(fl), fl, zonal[fl]))
            source = jnp.zeros((total, 256), F32)
            for i, offset in enumerate(range(-2, 4)):
                moved = pltpu.roll(value, (-offset) % total, 0) if offset else value
                source = source + weights[i] * moved
            phi = jnp.where(outside, 0.0, source)
            source = source * inverse
            for _ in range(SWEEPS):
                beside = pltpu.roll(phi, 1, 0) + pltpu.roll(phi, total - 1, 0)
                beside = beside + pltpu.roll(phi, 1, 1) + pltpu.roll(phi, 255, 1)
                phi = source + factor * beside
            out[f, l] = pltpu.roll(phi[8 : 8 + rows], 252, 1)[:, 0:128]


def call(kernel, shapes, limit=32, **more):
    return pl.pallas_call(
        kernel,
        out_shape=[jax.ShapeDtypeStruct(s, d) for s, d in shapes],
        compiler_params=pltpu.CompilerParams(vmem_limit_bytes=limit << 20),
        **more,
    )


def body(state, zonal_shift, zonal_cells, zonal_fraction, merid_cells, merid_fraction, coupling):
    rows = state.shape[2]
    bands = lax.axis_size("lat")
    coefs = (zonal_cells, zonal_fraction, merid_cells, merid_fraction, coupling)
    loads = (state, zonal_shift, *coefs)
    lat_pairs = [
        [i * SECTORS + s, (i + 1) * SECTORS + s] for i in range(0, bands, 2) for s in range(SECTORS)
    ]
    lat_swaps = [p for i in range(1, bands - 1, 2) for p in ((i, i + 1), (i + 1, i))]

    packed, begin = call(
        pack_kernel,
        [((4, 9, rows, 128), F32), ((2, rows, 128), I32)],
        60,
        scratch_shapes=[pltpu.VMEM(v.shape, v.dtype) for v in loads] + [pltpu.SemaphoreType.DMA((7,))],
        in_specs=[pl.BlockSpec(memory_space=pltpu.HBM)] * 7,
    )(*loads)
    ring = lax.all_to_all(packed, "lon", 0, 0, axis_index_groups=Y_RINGS)
    circle = lax.all_gather(ring, "lon", axis_index_groups=CORES)
    keep, send = call(window_kernel, [((10, rows, 128), F32)] * 2)(circle, begin)
    swapped = lax.all_gather(send, "lon", axis_index_groups=Z_PAIRS)
    zonal, coef, ea, eb = call(
        zonal_kernel,
        [((8, rows, 256), F32), ((6, rows, 256), F32), ((12, 8, 128), F32), ((12, 8, 128), F32)],
    )(keep, swapped, *coefs)
    gb = lax.ppermute(eb, "lat", lat_swaps)
    ga = lax.all_gather(ea, ("lat", "lon"), axis_index_groups=lat_pairs)
    (advanced,) = call(sweep_kernel, [(state.shape, F32)])(zonal, coef, ga, gb)
    return advanced


def solution(mesh):
    in_specs = (
        P(None, None, "lat", "lon"),
        P(None, "lat"),
        P(None, "lat", "lon"),
        P(None, "lat", "lon"),
        P(None, "lat", "lon"),
        P(None, "lat", "lon"),
        P(None, "lat", "lon"),
    )
    out_specs = P(None, None, "lat", "lon")
    return jax.shard_map(body, mesh=mesh, in_specs=in_specs, out_specs=out_specs, check_vma=False)
```

```python
import jax
import jax.numpy as jnp
from jax import lax
from jax.experimental import pallas as pl
from jax.experimental.pallas import tpu as pltpu
from jax.sharding import PartitionSpec as P

SWEEPS = 4
F32 = jnp.float32
I32 = jnp.int32
SECTORS = 16
Z_PAIRS = [[4 * y + c, 4 * y + 2 + c] for y in range(4) for c in range(2)]
Y_RINGS = [[4 * y + k for y in range(4)] for k in range(4)]
CORES = [[2 * i, 2 * i + 1] for i in range(SECTORS // 2)]


def iota(shape, dim):
    return lax.broadcasted_iota(I32, shape, dim)


def cubic_weights(frac):
    return (
        -frac * (frac - 1.0) * (frac - 2.0) / 6.0,
        (frac + 1.0) * (frac - 1.0) * (frac - 2.0) / 2.0,
        -(frac + 1.0) * frac * (frac - 2.0) / 2.0,
        (frac + 1.0) * frac * (frac - 1.0) / 6.0,
    )


def offset_weights(frac, cells, lowest, highest):
    w = cubic_weights(frac)
    result = []
    for offset in range(-1 - highest, 3 - lowest):
        total = jnp.zeros_like(frac)
        for k in range(4):
            c = k - 1 - offset
            if lowest <= c <= highest:
                total = jnp.where(cells == float(c), w[k], total)
        result.append(total)
    return result


def pack_rows(first, second, top):
    a = jnp.where(top, first, pltpu.roll(first, 4, 0))
    b = jnp.where(top, pltpu.roll(second, 4, 0), second)
    return jnp.where(iota((8, 128), 0) < 4, a, b)


def unpack_rows(packed):
    low = iota((8, 128), 0) < 4
    turned = pltpu.roll(packed, 4, 0)
    return jnp.where(low, packed, turned), jnp.where(low, turned, packed)


def fold(x):
    lane = iota((8, 128), 1)
    low, early = lane < 80, (lane & 7) < 4
    first = jnp.where(early, x[0:8], pltpu.roll(x[8:16], 4, 1))
    second = jnp.where(early, pltpu.roll(x[16:24], 80, 1), pltpu.roll(x[16:24], 36, 1))
    return jnp.where(low, first, second)


def unfold(x):
    lane = iota((8, 128), 1)
    third = jnp.where(lane < 48, pltpu.roll(x, 48, 1), pltpu.roll(x, 92, 1))
    return jnp.concatenate([x, pltpu.roll(x, 124, 1), third], axis=0)


def pack_kernel(state, *refs):
    sources, out, begin, held, plane, sems = refs[:6], refs[6], refs[7], refs[8:14], refs[14], refs[15]
    loads = [pltpu.make_async_copy(s, h, sems.at[i]) for i, (s, h) in enumerate(zip(sources, held))]
    blocks = [
        pltpu.make_async_copy(state, out.at[peer, pl.ds(0, 8)], sems.at[6 + peer]) for peer in range(4)
    ]
    for copy in loads + blocks:
        copy.start()
    for copy in loads:
        copy.wait()
    shift, coefs = held[0], held[1:]
    rows = state.shape[1]
    group = iota((rows, 128), 1) // 8
    edges = jnp.zeros((rows, 128), F32)
    for i, ref in enumerate(coefs):
        for l in range(2):
            a = 2 * i + l
            edges = jnp.where(group == a, pltpu.roll(ref[l].astype(F32), 8 * a + 4, 1), edges)
    plane[...] = edges
    planes = [pltpu.make_async_copy(plane, out.at[peer, 8], sems.at[10 + peer]) for peer in range(4)]
    for copy in planes:
        copy.start()
    eye = iota((rows, rows), 0) == iota((rows, rows), 1)
    for l in range(2):
        line = jnp.broadcast_to(shift[l : l + 1, :].astype(F32), (rows, rows))
        moved = jnp.sum(jnp.where(eye, line, 0.0), axis=1, keepdims=True).astype(I32)
        begin[l] = jnp.broadcast_to((-moved - 7) & 2047, (rows, 128))
    for copy in blocks + planes:
        copy.wait()


def window_kernel(circle, begin, keep, send):
    rows = circle.shape[3]
    me = lax.axis_index("lon")
    core, side = me & 1, me & 2
    lane = iota((rows, 128), 1)
    outs = (keep, send)
    slot = lane // 16
    tails = [jnp.zeros((rows, 128), F32) for _ in outs]
    for l in range(2):
        spot = (begin[l] & 127) + lane
        index, inside = spot & 127, spot < 128
        hops = begin[l] >> 7
        sectors = [((me ^ (2 * t)) + hops) & 15 for t in range(2)]
        for f in range(4):
            fl = 2 * f + l
            block = [[jnp.zeros((rows, 128), F32) for _ in range(3)] for _ in range(2)]
            for y in range(4):
                for c in range(2):
                    s = 4 * y + side + c
                    value = circle[c, y, fl]
                    for t in range(2):
                        for k in range(3):
                            hit = sectors[t] == ((s - k) & 15)
                            block[t][k] = jnp.where(hit, value, block[t][k])
            for t, out in enumerate(outs):
                r = [jnp.take_along_axis(v, index, axis=1) for v in block[t]]
                out[rows * fl : rows * fl + rows] = jnp.where(inside, r[0], r[1])
                tail = jnp.where(inside, r[1], r[2])
                tail = pltpu.roll(tail, 16 * fl, 1) if fl else tail
                tails[t] = jnp.where(slot == fl, tail, tails[t])
    for t, out in enumerate(outs):
        out[8 * rows : 9 * rows] = tails[t]
    keep[9 * rows : 10 * rows] = circle[1 - core, me // 4, 8]
    outer = ((me ^ 2) + jnp.where(core == 0, 15, 1)) & 15
    outer = circle[1 - core, outer // 4, 8]
    outer = jnp.where(core == 0, outer, pltpu.roll(outer, 124, 1))
    send[9 * rows : 9 * rows + 8] = fold(outer)


def zonal_kernel(keep, swapped, zc, zf, mc, mf, cp, out, ea, eb):
    rows = zc.shape[1]
    me, band = lax.axis_index("lon"), lax.axis_index("lat")
    core = me & 1
    across = 1 - ((me >> 1) & 1)
    lane = iota((rows, 128), 1)
    outer = unfold(swapped[across, 9 * rows : 9 * rows + 8])
    outer = jnp.where(core == 0, outer, pltpu.roll(outer, 4, 1))
    early = jnp.where((lane & 7) < 4, 0, 1)
    beside = jnp.where(early == core, outer, keep[9 * rows : 10 * rows])

    def both(plane):
        at = plane * rows
        return keep[at : at + rows] + swapped[across, at : at + rows]

    def extended(ref, i, l):
        a = 2 * i + l
        own = pltpu.roll(ref[l].astype(F32), 4, 1)
        side = pltpu.roll(beside, 128 - 8 * a, 1) if a else beside
        return jnp.where(lane < 4, side, own), jnp.where(lane < 4, own, side)

    ends = both(8)
    slot = lane // 8
    tails = jnp.zeros((rows, 128), F32)
    for l in range(2):
        cells, frac = [jnp.concatenate(extended(r, i, l), axis=1) for i, r in enumerate((zc, zf))]
        weights = offset_weights(frac, cells, -2, 2)
        for f in range(4):
            fl = 2 * f + l
            end = pltpu.roll(ends, 128 - 16 * fl, 1) if fl else ends
            window = jnp.concatenate([both(fl), end], axis=1)
            total = weights[0] * window
            for d in range(1, 8):
                total = total + weights[d] * pltpu.roll(window, 256 - d, 1)
            out[fl] = total[:, 0:128]
            tail = pltpu.roll(total[:, 128:256], 8 * fl, 1) if fl else total[:, 128:256]
            tails = jnp.where(slot == fl, tail, tails)
    for i, ref in enumerate((mc, mf, cp)):
        for l in range(2):
            a = 8 + 2 * i + l
            out[a + 1], tail = extended(ref, i + 2, l)
            tails = jnp.where(slot == a, pltpu.roll(tail, 8 * a, 1), tails)
    out[8] = tails

    even = (band & 1) == 0
    for e, top in ((ea, jnp.logical_not(even)), (eb, even)):
        take = pl.ds(pl.multiple_of(jnp.where(top, 0, rows - 8), 8), 8)
        for plane in range(9):
            e[plane] = out[plane, take]
        for i in range(3):
            e[9 + i] = pack_rows(out[9 + 2 * i, take], out[10 + 2 * i, take], top)


def sweep_kernel(main, ga, gb, result, done, sems):
    rows = main.shape[1]
    total = rows + 8
    band, bands = lax.axis_index("lat"), lax.axis_size("lat")
    even = (band & 1) == 0
    lane, row = iota((total, 128), 1), iota((total, 128), 0)
    outside = ((row < 4) & (band == 0)) | ((row >= rows + 4) & (band == bands - 1))
    tall = iota((rows + 16, 128), 0)
    beyond = ((tall < 8) & (band == 0)) | ((tall >= rows + 8) & (band == bands - 1))

    def pick(plane):
        above = jnp.where(even, gb[plane], ga[0, plane])
        below = jnp.where(even, ga[1, plane], gb[plane])
        return above, below

    def joined(ends, own):
        return jnp.concatenate([ends[0], own, ends[1]], axis=0)

    def rotated(x, lanes):
        return pltpu.roll(x, lanes % 128, 1) if lanes % 128 else x

    def prepare(cells, frac, coupling):
        weights = offset_weights(frac, cells, -1, 1)
        inverse = jnp.where(outside, 0.0, 1.0 / (1.0 + 4.0 * coupling))
        return weights, inverse, coupling * inverse

    def source_of(value, weights):
        value = jnp.where(beyond, 0.0, value)
        source = jnp.zeros((total, 128), F32)
        for i in range(6):
            moved = pltpu.roll(value, rows + 16 - (2 + i), 0)[:total]
            source = source + weights[i] * moved
        return jnp.where(outside, 0.0, source)

    packs = [[unpack_rows(v) for v in pick(9 + i)] for i in range(3)]
    tails = joined(pick(8), main[8])
    edge = pltpu.roll(tails, rows + 12, 0)[:total]
    group = []
    for i in range(3):
        v = rotated(edge, 64 - 16 * i)
        v = jnp.where(lane < 16, v, pltpu.roll(v, 16, 1))
        group.append(jnp.where(lane < 32, v, pltpu.roll(v, 32, 1)))
    weights, inverse, tail_factor = prepare(*group)
    tail = source_of(tails, weights)
    tail_source = tail * inverse
    phi, source, factor = [None] * 8, [None] * 8, [None] * 8
    for l in range(2):
        coefs = []
        for i in range(3):
            own = joined([v[l] for v in packs[i]], main[9 + 2 * i + l])
            coefs.append(pltpu.roll(own, rows + 12, 0)[:total])
        weights, inverse, level_factor = prepare(*coefs)
        for f in range(4):
            fl = 2 * f + l
            value = source_of(joined(pick(fl), main[fl]), weights)
            phi[fl] = rotated(value, 8 * fl)
            source[fl] = rotated(value * inverse, 8 * fl)
            factor[fl] = rotated(level_factor, 8 * fl)
    for sweep in range(SWEEPS):
        old_tail = tail
        tail_left, tail_right = pltpu.roll(tail, 1, 1), pltpu.roll(tail, 127, 1)
        for fl in range(8):
            old = phi[fl]
            left = pltpu.roll(old, 1, 1)
            tail_left = jnp.where(lane == 8 * fl, left, tail_left)
            right = jnp.where(lane == (8 * fl - 1) % 128, tail_right, pltpu.roll(old, 127, 1))
            beside = pltpu.roll(old, 1, 0) + pltpu.roll(old, total - 1, 0) + left + right
            phi[fl] = source[fl] + factor[fl] * beside
        beside = pltpu.roll(old_tail, 1, 0) + pltpu.roll(old_tail, total - 1, 0)
        tail = tail_source + tail_factor * (beside + tail_left + tail_right)
    copies = []
    for fl in range(8):
        whole = jnp.where((lane >= 8 * fl) & (lane < 8 * fl + 4), tail, phi[fl])
        whole = rotated(whole, -4 - 8 * fl)
        done[fl] = pltpu.roll(whole, total - 4, 0)[:rows]
        copies.append(pltpu.make_async_copy(done.at[fl], result.at[fl], sems.at[fl]))
        copies[-1].start()
    for copy in copies:
        copy.wait()


def call(kernel, shapes, limit=32, **more):
    return pl.pallas_call(
        kernel,
        out_shape=[jax.ShapeDtypeStruct(s, d) for s, d in shapes],
        compiler_params=pltpu.CompilerParams(vmem_limit_bytes=limit << 20),
        **more,
    )


def body(state, zonal_shift, zonal_cells, zonal_fraction, merid_cells, merid_fraction, coupling):
    rows = state.shape[2]
    bands = lax.axis_size("lat")
    coefs = (zonal_cells, zonal_fraction, merid_cells, merid_fraction, coupling)
    loads = (state, zonal_shift, *coefs)
    lat_pairs = [
        [i * SECTORS + s, (i + 1) * SECTORS + s] for i in range(0, bands, 2) for s in range(SECTORS)
    ]
    lat_swaps = [p for i in range(1, bands - 1, 2) for p in ((i, i + 1), (i + 1, i))]

    hbm = pl.BlockSpec(memory_space=pltpu.HBM)
    vmem = pl.BlockSpec(memory_space=pltpu.VMEM)
    packed, begin = call(
        pack_kernel,
        [((4, 9, rows, 128), F32), ((2, rows, 128), I32)],
        60,
        scratch_shapes=[pltpu.VMEM(v.shape, v.dtype) for v in loads[1:]]
        + [pltpu.VMEM((rows, 128), F32), pltpu.SemaphoreType.DMA((14,))],
        in_specs=[hbm] * 7,
        out_specs=[hbm, vmem],
    )(state.reshape(8, rows, 128), *loads[1:])
    ring = lax.all_to_all(packed, "lon", 0, 0, axis_index_groups=Y_RINGS)
    circle = lax.all_gather(ring, "lon", axis_index_groups=CORES)
    keep, send = call(
        window_kernel, [((10 * rows, 128), F32), ((9 * rows + 8, 128), F32)]
    )(circle, begin)
    swapped = lax.all_gather(send, "lon", axis_index_groups=Z_PAIRS)
    main, ea, eb = call(
        zonal_kernel, [((15, rows, 128), F32), ((12, 8, 128), F32), ((12, 8, 128), F32)]
    )(keep, swapped, *coefs)
    gb = lax.ppermute(eb, "lat", lat_swaps)
    ga = lax.all_gather(ea, ("lat", "lon"), axis_index_groups=lat_pairs)
    (advanced,) = call(
        sweep_kernel,
        [((8, rows, 128), F32)],
        scratch_shapes=[pltpu.VMEM((8, rows, 128), F32), pltpu.SemaphoreType.DMA((8,))],
        out_specs=[hbm],
    )(main, ga, gb)
    return advanced.reshape(state.shape)


def solution(mesh):
    in_specs = (
        P(None, None, "lat", "lon"),
        P(None, "lat"),
        P(None, "lat", "lon"),
        P(None, "lat", "lon"),
        P(None, "lat", "lon"),
        P(None, "lat", "lon"),
        P(None, "lat", "lon"),
    )
    out_specs = P(None, None, "lat", "lon")
    return jax.shard_map(body, mesh=mesh, in_specs=in_specs, out_specs=out_specs, check_vma=False)
```

```python
import jax
import jax.numpy as jnp
from jax import lax
from jax.experimental import pallas as pl
from jax.experimental.pallas import tpu as pltpu
from jax.sharding import PartitionSpec as P

SWEEPS = 4
F32 = jnp.float32
I32 = jnp.int32
SECTORS = 16
Z_PAIRS = [[4 * y + c, 4 * y + 2 + c] for y in range(4) for c in range(2)]
Y_RINGS = [[4 * y + k for y in range(4)] for k in range(4)]
CORES = [[2 * i, 2 * i + 1] for i in range(SECTORS // 2)]


def iota(shape, dim):
    return lax.broadcasted_iota(I32, shape, dim)


def cubic_weights(frac):
    return (
        -frac * (frac - 1.0) * (frac - 2.0) / 6.0,
        (frac + 1.0) * (frac - 1.0) * (frac - 2.0) / 2.0,
        -(frac + 1.0) * frac * (frac - 2.0) / 2.0,
        (frac + 1.0) * frac * (frac - 1.0) / 6.0,
    )


def offset_weights(frac, cells, lowest, highest):
    w = cubic_weights(frac)
    result = []
    for offset in range(-1 - highest, 3 - lowest):
        total = jnp.zeros_like(frac)
        for k in range(4):
            c = k - 1 - offset
            if lowest <= c <= highest:
                total = jnp.where(cells == float(c), w[k], total)
        result.append(total)
    return result


def pack_rows(first, second, top):
    a = jnp.where(top, first, pltpu.roll(first, 4, 0))
    b = jnp.where(top, pltpu.roll(second, 4, 0), second)
    return jnp.where(iota((8, 128), 0) < 4, a, b)


def unpack_rows(packed):
    low = iota((8, 128), 0) < 4
    turned = pltpu.roll(packed, 4, 0)
    return jnp.where(low, packed, turned), jnp.where(low, turned, packed)


def fold(x):
    lane = iota((8, 128), 1)
    low, early = lane < 80, (lane & 7) < 4
    first = jnp.where(early, x[0:8], pltpu.roll(x[8:16], 4, 1))
    second = jnp.where(early, pltpu.roll(x[16:24], 80, 1), pltpu.roll(x[16:24], 36, 1))
    return jnp.where(low, first, second)


def unfold(x):
    lane = iota((8, 128), 1)
    third = jnp.where(lane < 48, pltpu.roll(x, 48, 1), pltpu.roll(x, 92, 1))
    return jnp.concatenate([x, pltpu.roll(x, 124, 1), third], axis=0)


def pack_kernel(*refs):
    sources, out, begin, held, sems = refs[:7], refs[7], refs[8], refs[9:16], refs[16]
    loads = [pltpu.make_async_copy(s, h, sems.at[i]) for i, (s, h) in enumerate(zip(sources, held))]
    for copy in loads:
        copy.start()
    for copy in loads[1:]:
        copy.wait()
    state, shift, coefs = held[0], held[1], held[2:]
    rows = state.shape[1]
    group = iota((rows, 128), 1) // 8
    edges = jnp.zeros((rows, 128), F32)
    for i, ref in enumerate(coefs):
        for l in range(2):
            a = 2 * i + l
            edges = jnp.where(group == a, pltpu.roll(ref[l].astype(F32), 8 * a + 4, 1), edges)
    eye = iota((rows, rows), 0) == iota((rows, rows), 1)
    for l in range(2):
        line = jnp.broadcast_to(shift[l : l + 1, :].astype(F32), (rows, rows))
        moved = jnp.sum(jnp.where(eye, line, 0.0), axis=1, keepdims=True).astype(I32)
        begin[l] = jnp.broadcast_to((-moved - 7) & 2047, (rows, 128))
    loads[0].wait()
    for fl in range(8):
        for peer in range(4):
            out[peer, fl] = state[fl]
    for peer in range(4):
        out[peer, 8] = edges


def window_kernel(circle, begin, keep, send):
    rows = circle.shape[3]
    me = lax.axis_index("lon")
    core, side = me & 1, me & 2
    lane = iota((rows, 128), 1)
    outs = (keep, send)
    slot = lane // 16
    tails = [jnp.zeros((rows, 128), F32) for _ in outs]
    for l in range(2):
        spot = (begin[l] & 127) + lane
        index, inside = spot & 127, spot < 128
        hops = begin[l] >> 7
        sectors = [((me ^ (2 * t)) + hops) & 15 for t in range(2)]
        for f in range(4):
            fl = 2 * f + l
            block = [[jnp.zeros((rows, 128), F32) for _ in range(3)] for _ in range(2)]
            for y in range(4):
                for c in range(2):
                    s = 4 * y + side + c
                    value = circle[c, y, fl]
                    for t in range(2):
                        for k in range(3):
                            hit = sectors[t] == ((s - k) & 15)
                            block[t][k] = jnp.where(hit, value, block[t][k])
            for t, out in enumerate(outs):
                r = [jnp.take_along_axis(v, index, axis=1) for v in block[t]]
                out[rows * fl : rows * fl + rows] = jnp.where(inside, r[0], r[1])
                tail = jnp.where(inside, r[1], r[2])
                tail = pltpu.roll(tail, 16 * fl, 1) if fl else tail
                tails[t] = jnp.where(slot == fl, tail, tails[t])
    for t, out in enumerate(outs):
        out[8 * rows : 9 * rows] = tails[t]
    keep[9 * rows : 10 * rows] = circle[1 - core, me // 4, 8]
    outer = ((me ^ 2) + jnp.where(core == 0, 15, 1)) & 15
    outer = circle[1 - core, outer // 4, 8]
    outer = jnp.where(core == 0, outer, pltpu.roll(outer, 124, 1))
    send[9 * rows : 9 * rows + 8] = fold(outer)


def zonal_kernel(keep, swapped, zc, zf, mc, mf, cp, out, ea, eb):
    rows = zc.shape[1]
    me, band = lax.axis_index("lon"), lax.axis_index("lat")
    core = me & 1
    across = 1 - ((me >> 1) & 1)
    lane = iota((rows, 128), 1)
    outer = unfold(swapped[across, 9 * rows : 9 * rows + 8])
    outer = jnp.where(core == 0, outer, pltpu.roll(outer, 4, 1))
    early = jnp.where((lane & 7) < 4, 0, 1)
    beside = jnp.where(early == core, outer, keep[9 * rows : 10 * rows])

    def both(plane):
        at = plane * rows
        return keep[at : at + rows] + swapped[across, at : at + rows]

    def extended(ref, i, l):
        a = 2 * i + l
        own = pltpu.roll(ref[l].astype(F32), 4, 1)
        side = pltpu.roll(beside, 128 - 8 * a, 1) if a else beside
        return jnp.where(lane < 4, side, own), jnp.where(lane < 4, own, side)

    ends = both(8)
    slot = lane // 8
    tails = jnp.zeros((rows, 128), F32)
    for l in range(2):
        cells, frac = [jnp.concatenate(extended(r, i, l), axis=1) for i, r in enumerate((zc, zf))]
        weights = offset_weights(frac, cells, -2, 2)
        for f in range(4):
            fl = 2 * f + l
            end = pltpu.roll(ends, 128 - 16 * fl, 1) if fl else ends
            window = jnp.concatenate([both(fl), end], axis=1)
            total = weights[0] * window
            for d in range(1, 8):
                total = total + weights[d] * pltpu.roll(window, 256 - d, 1)
            out[fl] = total[:, 0:128]
            tail = pltpu.roll(total[:, 128:256], 8 * fl, 1) if fl else total[:, 128:256]
            tails = jnp.where(slot == fl, tail, tails)
    for i, ref in enumerate((mc, mf, cp)):
        for l in range(2):
            a = 8 + 2 * i + l
            out[a + 1], tail = extended(ref, i + 2, l)
            tails = jnp.where(slot == a, pltpu.roll(tail, 8 * a, 1), tails)
    out[8] = tails

    even = (band & 1) == 0
    for e, top in ((ea, jnp.logical_not(even)), (eb, even)):
        take = pl.ds(pl.multiple_of(jnp.where(top, 0, rows - 8), 8), 8)
        for plane in range(9):
            e[plane] = out[plane, take]
        for i in range(3):
            e[9 + i] = pack_rows(out[9 + 2 * i, take], out[10 + 2 * i, take], top)


def sweep_kernel(main, ga, gb, result, done, sems):
    rows = main.shape[1]
    total = rows + 8
    band, bands = lax.axis_index("lat"), lax.axis_size("lat")
    even = (band & 1) == 0
    lane, row = iota((total, 128), 1), iota((total, 128), 0)
    outside = ((row < 4) & (band == 0)) | ((row >= rows + 4) & (band == bands - 1))
    tall = iota((rows + 16, 128), 0)
    beyond = ((tall < 8) & (band == 0)) | ((tall >= rows + 8) & (band == bands - 1))

    def pick(plane):
        above = jnp.where(even, gb[plane], ga[0, plane])
        below = jnp.where(even, ga[1, plane], gb[plane])
        return above, below

    def joined(ends, own):
        return jnp.concatenate([ends[0], own, ends[1]], axis=0)

    def rotated(x, lanes):
        return pltpu.roll(x, lanes % 128, 1) if lanes % 128 else x

    def prepare(cells, frac, coupling):
        weights = offset_weights(frac, cells, -1, 1)
        inverse = jnp.where(outside, 0.0, 1.0 / (1.0 + 4.0 * coupling))
        return weights, inverse, coupling * inverse

    def source_of(value, weights):
        value = jnp.where(beyond, 0.0, value)
        source = jnp.zeros((total, 128), F32)
        for i in range(6):
            moved = pltpu.roll(value, rows + 16 - (2 + i), 0)[:total]
            source = source + weights[i] * moved
        return jnp.where(outside, 0.0, source)

    packs = [[unpack_rows(v) for v in pick(9 + i)] for i in range(3)]
    tails = joined(pick(8), main[8])
    edge = pltpu.roll(tails, rows + 12, 0)[:total]
    group = []
    for i in range(3):
        v = rotated(edge, 64 - 16 * i)
        v = jnp.where(lane < 16, v, pltpu.roll(v, 16, 1))
        group.append(jnp.where(lane < 32, v, pltpu.roll(v, 32, 1)))
    weights, inverse, tail_factor = prepare(*group)
    tail = source_of(tails, weights)
    tail_source = tail * inverse
    phi, source, factor = [None] * 8, [None] * 8, [None] * 8
    for l in range(2):
        coefs = []
        for i in range(3):
            own = joined([v[l] for v in packs[i]], main[9 + 2 * i + l])
            coefs.append(pltpu.roll(own, rows + 12, 0)[:total])
        weights, inverse, level_factor = prepare(*coefs)
        for f in range(4):
            fl = 2 * f + l
            value = source_of(joined(pick(fl), main[fl]), weights)
            phi[fl] = rotated(value, 8 * fl)
            source[fl] = rotated(value * inverse, 8 * fl)
            factor[fl] = rotated(level_factor, 8 * fl)
    for sweep in range(SWEEPS):
        old_tail = tail
        tail_left, tail_right = pltpu.roll(tail, 1, 1), pltpu.roll(tail, 127, 1)
        for fl in range(8):
            old = phi[fl]
            left = pltpu.roll(old, 1, 1)
            tail_left = jnp.where(lane == 8 * fl, left, tail_left)
            right = jnp.where(lane == (8 * fl - 1) % 128, tail_right, pltpu.roll(old, 127, 1))
            beside = pltpu.roll(old, 1, 0) + pltpu.roll(old, total - 1, 0) + left + right
            phi[fl] = source[fl] + factor[fl] * beside
        beside = pltpu.roll(old_tail, 1, 0) + pltpu.roll(old_tail, total - 1, 0)
        tail = tail_source + tail_factor * (beside + tail_left + tail_right)
    copies = []
    for fl in range(8):
        whole = jnp.where((lane >= 8 * fl) & (lane < 8 * fl + 4), tail, phi[fl])
        whole = rotated(whole, -4 - 8 * fl)
        done[fl] = pltpu.roll(whole, total - 4, 0)[:rows]
        copies.append(pltpu.make_async_copy(done.at[fl], result.at[fl], sems.at[fl]))
        copies[-1].start()
    for copy in copies:
        copy.wait()


def call(kernel, shapes, limit=32, **more):
    return pl.pallas_call(
        kernel,
        out_shape=[jax.ShapeDtypeStruct(s, d) for s, d in shapes],
        compiler_params=pltpu.CompilerParams(vmem_limit_bytes=limit << 20),
        **more,
    )


def body(state, zonal_shift, zonal_cells, zonal_fraction, merid_cells, merid_fraction, coupling):
    rows = state.shape[2]
    bands = lax.axis_size("lat")
    coefs = (zonal_cells, zonal_fraction, merid_cells, merid_fraction, coupling)
    loads = (state.reshape(8, rows, 128), zonal_shift, *coefs)
    lat_pairs = [
        [i * SECTORS + s, (i + 1) * SECTORS + s] for i in range(0, bands, 2) for s in range(SECTORS)
    ]
    lat_swaps = [p for i in range(1, bands - 1, 2) for p in ((i, i + 1), (i + 1, i))]

    hbm = pl.BlockSpec(memory_space=pltpu.HBM)
    packed, begin = call(
        pack_kernel,
        [((4, 9, rows, 128), F32), ((2, rows, 128), I32)],
        60,
        scratch_shapes=[pltpu.VMEM(v.shape, v.dtype) for v in loads]
        + [pltpu.SemaphoreType.DMA((7,))],
        in_specs=[hbm] * 7,
    )(*loads)
    ring = lax.all_to_all(packed, "lon", 0, 0, axis_index_groups=Y_RINGS)
    circle = lax.all_gather(ring, "lon", axis_index_groups=CORES)
    keep, send = call(
        window_kernel, [((10 * rows, 128), F32), ((9 * rows + 8, 128), F32)]
    )(circle, begin)
    swapped = lax.all_gather(send, "lon", axis_index_groups=Z_PAIRS)
    main, ea, eb = call(
        zonal_kernel, [((15, rows, 128), F32), ((12, 8, 128), F32), ((12, 8, 128), F32)]
    )(keep, swapped, *coefs)
    gb = lax.ppermute(eb, "lat", lat_swaps)
    ga = lax.all_gather(ea, ("lat", "lon"), axis_index_groups=lat_pairs)
    (advanced,) = call(
        sweep_kernel,
        [((8, rows, 128), F32)],
        scratch_shapes=[pltpu.VMEM((8, rows, 128), F32), pltpu.SemaphoreType.DMA((8,))],
        out_specs=[hbm],
    )(main, ga, gb)
    return advanced.reshape(state.shape)


def solution(mesh):
    in_specs = (
        P(None, None, "lat", "lon"),
        P(None, "lat"),
        P(None, "lat", "lon"),
        P(None, "lat", "lon"),
        P(None, "lat", "lon"),
        P(None, "lat", "lon"),
        P(None, "lat", "lon"),
    )
    out_specs = P(None, None, "lat", "lon")
    return jax.shard_map(body, mesh=mesh, in_specs=in_specs, out_specs=out_specs, check_vma=False)
```

```python
import jax
import jax.numpy as jnp
from jax import lax
from jax.experimental import pallas as pl
from jax.experimental.pallas import tpu as pltpu
from jax.sharding import PartitionSpec as P

SWEEPS = 4
F32 = jnp.float32
I32 = jnp.int32
SECTORS = 16
Z_PAIRS = [[4 * y + c, 4 * y + 2 + c] for y in range(4) for c in range(2)]
SIDES = [[4 * y + 2 * z + c for y in range(4) for c in range(2)] for z in range(2)]


def iota(shape, dim):
    return lax.broadcasted_iota(I32, shape, dim)


def cubic_weights(frac):
    return (
        -frac * (frac - 1.0) * (frac - 2.0) / 6.0,
        (frac + 1.0) * (frac - 1.0) * (frac - 2.0) / 2.0,
        -(frac + 1.0) * frac * (frac - 2.0) / 2.0,
        (frac + 1.0) * frac * (frac - 1.0) / 6.0,
    )


def offset_weights(frac, cells, lowest, highest):
    w = cubic_weights(frac)
    result = []
    for offset in range(-1 - highest, 3 - lowest):
        total = jnp.zeros_like(frac)
        for k in range(4):
            c = k - 1 - offset
            if lowest <= c <= highest:
                total = jnp.where(cells == float(c), w[k], total)
        result.append(total)
    return result


def pack_rows(first, second, top):
    a = jnp.where(top, first, pltpu.roll(first, 4, 0))
    b = jnp.where(top, pltpu.roll(second, 4, 0), second)
    return jnp.where(iota((8, 128), 0) < 4, a, b)


def unpack_rows(packed):
    low = iota((8, 128), 0) < 4
    turned = pltpu.roll(packed, 4, 0)
    return jnp.where(low, packed, turned), jnp.where(low, turned, packed)


def fold(x):
    lane = iota((8, 128), 1)
    low, early = lane < 80, (lane & 7) < 4
    first = jnp.where(early, x[0:8], pltpu.roll(x[8:16], 4, 1))
    second = jnp.where(early, pltpu.roll(x[16:24], 80, 1), pltpu.roll(x[16:24], 36, 1))
    return jnp.where(low, first, second)


def unfold(x):
    lane = iota((8, 128), 1)
    third = jnp.where(lane < 48, pltpu.roll(x, 48, 1), pltpu.roll(x, 92, 1))
    return jnp.concatenate([x, pltpu.roll(x, 124, 1), third], axis=0)


def pack_kernel(*refs):
    sources, out, begin, held, sems = refs[:7], refs[7], refs[8], refs[9:16], refs[16]
    loads = [pltpu.make_async_copy(s, h, sems.at[i]) for i, (s, h) in enumerate(zip(sources, held))]
    for copy in loads:
        copy.start()
    for copy in loads[1:]:
        copy.wait()
    state, shift, coefs = held[0], held[1], held[2:]
    rows = state.shape[1]
    group = iota((rows, 128), 1) // 8
    edges = jnp.zeros((rows, 128), F32)
    for i, ref in enumerate(coefs):
        for l in range(2):
            a = 2 * i + l
            edges = jnp.where(group == a, pltpu.roll(ref[l].astype(F32), 8 * a + 4, 1), edges)
    eye = iota((rows, rows), 0) == iota((rows, rows), 1)
    for l in range(2):
        line = jnp.broadcast_to(shift[l : l + 1, :].astype(F32), (rows, rows))
        moved = jnp.sum(jnp.where(eye, line, 0.0), axis=1, keepdims=True).astype(I32)
        begin[l] = jnp.broadcast_to((-moved - 7) & 2047, (rows, 128))
    loads[0].wait()
    for fl in range(8):
        out[fl] = state[fl]
    out[8] = edges


def window_kernel(circle, begin, keep, send):
    rows = circle.shape[2]
    me = lax.axis_index("lon")
    core, side = me & 1, me & 2
    lane = iota((rows, 128), 1)
    outs = (keep, send)
    slot = lane // 16
    tails = [jnp.zeros((rows, 128), F32) for _ in outs]
    for l in range(2):
        spot = (begin[l] & 127) + lane
        index, inside = spot & 127, spot < 128
        hops = begin[l] >> 7
        sectors = [((me ^ (2 * t)) + hops) & 15 for t in range(2)]
        for f in range(4):
            fl = 2 * f + l
            block = [[jnp.zeros((rows, 128), F32) for _ in range(3)] for _ in range(2)]
            for y in range(4):
                for c in range(2):
                    s = 4 * y + side + c
                    value = circle[2 * y + c, fl]
                    for t in range(2):
                        for k in range(3):
                            hit = sectors[t] == ((s - k) & 15)
                            block[t][k] = jnp.where(hit, value, block[t][k])
            for t, out in enumerate(outs):
                r = [jnp.take_along_axis(v, index, axis=1) for v in block[t]]
                out[rows * fl : rows * fl + rows] = jnp.where(inside, r[0], r[1])
                tail = jnp.where(inside, r[1], r[2])
                tail = pltpu.roll(tail, 16 * fl, 1) if fl else tail
                tails[t] = jnp.where(slot == fl, tail, tails[t])
    for t, out in enumerate(outs):
        out[8 * rows : 9 * rows] = tails[t]
    keep[9 * rows : 10 * rows] = circle[me // 4 * 2 + 1 - core, 8]
    outer = ((me ^ 2) + jnp.where(core == 0, 15, 1)) & 15
    outer = circle[outer // 4 * 2 + 1 - core, 8]
    outer = jnp.where(core == 0, outer, pltpu.roll(outer, 124, 1))
    send[9 * rows : 9 * rows + 8] = fold(outer)


def zonal_kernel(keep, swapped, zc, zf, mc, mf, cp, out, ea, eb):
    rows = zc.shape[1]
    me, band = lax.axis_index("lon"), lax.axis_index("lat")
    core = me & 1
    across = 1 - ((me >> 1) & 1)
    lane = iota((rows, 128), 1)
    outer = unfold(swapped[across, 9 * rows : 9 * rows + 8])
    outer = jnp.where(core == 0, outer, pltpu.roll(outer, 4, 1))
    early = jnp.where((lane & 7) < 4, 0, 1)
    beside = jnp.where(early == core, outer, keep[9 * rows : 10 * rows])

    def both(plane):
        at = plane * rows
        return keep[at : at + rows] + swapped[across, at : at + rows]

    def extended(ref, i, l):
        a = 2 * i + l
        own = pltpu.roll(ref[l].astype(F32), 4, 1)
        side = pltpu.roll(beside, 128 - 8 * a, 1) if a else beside
        return jnp.where(lane < 4, side, own), jnp.where(lane < 4, own, side)

    ends = both(8)
    slot = lane // 8
    tails = jnp.zeros((rows, 128), F32)
    for l in range(2):
        cells, frac = [jnp.concatenate(extended(r, i, l), axis=1) for i, r in enumerate((zc, zf))]
        weights = offset_weights(frac, cells, -2, 2)
        for f in range(4):
            fl = 2 * f + l
            end = pltpu.roll(ends, 128 - 16 * fl, 1) if fl else ends
            window = jnp.concatenate([both(fl), end], axis=1)
            total = weights[0] * window
            for d in range(1, 8):
                total = total + weights[d] * pltpu.roll(window, 256 - d, 1)
            out[fl] = total[:, 0:128]
            tail = pltpu.roll(total[:, 128:256], 8 * fl, 1) if fl else total[:, 128:256]
            tails = jnp.where(slot == fl, tail, tails)
    for i, ref in enumerate((mc, mf, cp)):
        for l in range(2):
            a = 8 + 2 * i + l
            out[a + 1], tail = extended(ref, i + 2, l)
            tails = jnp.where(slot == a, pltpu.roll(tail, 8 * a, 1), tails)
    out[8] = tails

    even = (band & 1) == 0
    for e, top in ((ea, jnp.logical_not(even)), (eb, even)):
        take = pl.ds(pl.multiple_of(jnp.where(top, 0, rows - 8), 8), 8)
        for plane in range(9):
            e[plane] = out[plane, take]
        for i in range(3):
            e[9 + i] = pack_rows(out[9 + 2 * i, take], out[10 + 2 * i, take], top)


def sweep_kernel(main, ga, gb, result, done, sems):
    rows = main.shape[1]
    total = rows + 8
    band, bands = lax.axis_index("lat"), lax.axis_size("lat")
    even = (band & 1) == 0
    lane, row = iota((total, 128), 1), iota((total, 128), 0)
    outside = ((row < 4) & (band == 0)) | ((row >= rows + 4) & (band == bands - 1))
    tall = iota((rows + 16, 128), 0)
    beyond = ((tall < 8) & (band == 0)) | ((tall >= rows + 8) & (band == bands - 1))

    def pick(plane):
        above = jnp.where(even, gb[plane], ga[0, plane])
        below = jnp.where(even, ga[1, plane], gb[plane])
        return above, below

    def joined(ends, own):
        return jnp.concatenate([ends[0], own, ends[1]], axis=0)

    def rotated(x, lanes):
        return pltpu.roll(x, lanes % 128, 1) if lanes % 128 else x

    def prepare(cells, frac, coupling):
        weights = offset_weights(frac, cells, -1, 1)
        inverse = jnp.where(outside, 0.0, 1.0 / (1.0 + 4.0 * coupling))
        return weights, inverse, coupling * inverse

    def source_of(value, weights):
        value = jnp.where(beyond, 0.0, value)
        source = jnp.zeros((total, 128), F32)
        for i in range(6):
            moved = pltpu.roll(value, rows + 16 - (2 + i), 0)[:total]
            source = source + weights[i] * moved
        return jnp.where(outside, 0.0, source)

    packs = [[unpack_rows(v) for v in pick(9 + i)] for i in range(3)]
    tails = joined(pick(8), main[8])
    edge = pltpu.roll(tails, rows + 12, 0)[:total]
    group = []
    for i in range(3):
        v = rotated(edge, 64 - 16 * i)
        v = jnp.where(lane < 16, v, pltpu.roll(v, 16, 1))
        group.append(jnp.where(lane < 32, v, pltpu.roll(v, 32, 1)))
    weights, inverse, tail_factor = prepare(*group)
    tail = source_of(tails, weights)
    tail_source = tail * inverse
    phi, source, factor = [None] * 8, [None] * 8, [None] * 8
    for l in range(2):
        coefs = []
        for i in range(3):
            own = joined([v[l] for v in packs[i]], main[9 + 2 * i + l])
            coefs.append(pltpu.roll(own, rows + 12, 0)[:total])
        weights, inverse, level_factor = prepare(*coefs)
        for f in range(4):
            fl = 2 * f + l
            value = source_of(joined(pick(fl), main[fl]), weights)
            phi[fl] = rotated(value, 8 * fl)
            source[fl] = rotated(value * inverse, 8 * fl)
            factor[fl] = rotated(level_factor, 8 * fl)
    for sweep in range(SWEEPS):
        old_tail = tail
        tail_left, tail_right = pltpu.roll(tail, 1, 1), pltpu.roll(tail, 127, 1)
        for fl in range(8):
            old = phi[fl]
            left = pltpu.roll(old, 1, 1)
            tail_left = jnp.where(lane == 8 * fl, left, tail_left)
            right = jnp.where(lane == (8 * fl - 1) % 128, tail_right, pltpu.roll(old, 127, 1))
            beside = pltpu.roll(old, 1, 0) + pltpu.roll(old, total - 1, 0) + left + right
            phi[fl] = source[fl] + factor[fl] * beside
        beside = pltpu.roll(old_tail, 1, 0) + pltpu.roll(old_tail, total - 1, 0)
        tail = tail_source + tail_factor * (beside + tail_left + tail_right)
    copies = []
    for fl in range(8):
        whole = jnp.where((lane >= 8 * fl) & (lane < 8 * fl + 4), tail, phi[fl])
        whole = rotated(whole, -4 - 8 * fl)
        done[fl] = pltpu.roll(whole, total - 4, 0)[:rows]
        copies.append(pltpu.make_async_copy(done.at[fl], result.at[fl], sems.at[fl]))
        copies[-1].start()
    for copy in copies:
        copy.wait()


def call(kernel, shapes, limit=32, **more):
    return pl.pallas_call(
        kernel,
        out_shape=[jax.ShapeDtypeStruct(s, d) for s, d in shapes],
        compiler_params=pltpu.CompilerParams(vmem_limit_bytes=limit << 20),
        **more,
    )


def body(state, zonal_shift, zonal_cells, zonal_fraction, merid_cells, merid_fraction, coupling):
    rows = state.shape[2]
    bands = lax.axis_size("lat")
    coefs = (zonal_cells, zonal_fraction, merid_cells, merid_fraction, coupling)
    loads = (state.reshape(8, rows, 128), zonal_shift, *coefs)
    lat_pairs = [
        [i * SECTORS + s, (i + 1) * SECTORS + s] for i in range(0, bands, 2) for s in range(SECTORS)
    ]
    lat_swaps = [p for i in range(1, bands - 1, 2) for p in ((i, i + 1), (i + 1, i))]

    hbm = pl.BlockSpec(memory_space=pltpu.HBM)
    packed, begin = call(
        pack_kernel,
        [((9, rows, 128), F32), ((2, rows, 128), I32)],
        60,
        scratch_shapes=[pltpu.VMEM(v.shape, v.dtype) for v in loads]
        + [pltpu.SemaphoreType.DMA((7,))],
        in_specs=[hbm] * 7,
    )(*loads)
    circle = lax.all_gather(packed, "lon", axis_index_groups=SIDES)
    keep, send = call(
        window_kernel, [((10 * rows, 128), F32), ((9 * rows + 8, 128), F32)]
    )(circle, begin)
    swapped = lax.all_gather(send, "lon", axis_index_groups=Z_PAIRS)
    main, ea, eb = call(
        zonal_kernel, [((15, rows, 128), F32), ((12, 8, 128), F32), ((12, 8, 128), F32)]
    )(keep, swapped, *coefs)
    gb = lax.ppermute(eb, "lat", lat_swaps)
    ga = lax.all_gather(ea, ("lat", "lon"), axis_index_groups=lat_pairs)
    (advanced,) = call(
        sweep_kernel,
        [((8, rows, 128), F32)],
        scratch_shapes=[pltpu.VMEM((8, rows, 128), F32), pltpu.SemaphoreType.DMA((8,))],
        out_specs=[hbm],
    )(main, ga, gb)
    return advanced.reshape(state.shape)


def solution(mesh):
    in_specs = (
        P(None, None, "lat", "lon"),
        P(None, "lat"),
        P(None, "lat", "lon"),
        P(None, "lat", "lon"),
        P(None, "lat", "lon"),
        P(None, "lat", "lon"),
        P(None, "lat", "lon"),
    )
    out_specs = P(None, None, "lat", "lon")
    return jax.shard_map(body, mesh=mesh, in_specs=in_specs, out_specs=out_specs, check_vma=False)
```

```python
from functools import partial

import jax
import jax.numpy as jnp
from jax import lax
from jax.experimental import pallas as pl
from jax.experimental.pallas import tpu as pltpu
from jax.sharding import PartitionSpec as P

SWEEPS = 4
F32 = jnp.float32
I32 = jnp.int32
SECTORS = 16
Z_PAIRS = [[4 * y + c, 4 * y + 2 + c] for y in range(4) for c in range(2)]
SIDES = [[4 * y + 2 * z + c for y in range(4) for c in range(2)] for z in range(2)]


def iota(shape, dim):
    return lax.broadcasted_iota(I32, shape, dim)


def cubic_weights(frac):
    return (
        -frac * (frac - 1.0) * (frac - 2.0) / 6.0,
        (frac + 1.0) * (frac - 1.0) * (frac - 2.0) / 2.0,
        -(frac + 1.0) * frac * (frac - 2.0) / 2.0,
        (frac + 1.0) * frac * (frac - 1.0) / 6.0,
    )


def offset_weights(frac, cells, lowest, highest):
    w = cubic_weights(frac)
    result = []
    for offset in range(-1 - highest, 3 - lowest):
        total = jnp.zeros_like(frac)
        for k in range(4):
            c = k - 1 - offset
            if lowest <= c <= highest:
                total = jnp.where(cells == float(c), w[k], total)
        result.append(total)
    return result


def pack_rows(first, second, top):
    a = jnp.where(top, first, pltpu.roll(first, 4, 0))
    b = jnp.where(top, pltpu.roll(second, 4, 0), second)
    return jnp.where(iota((8, 128), 0) < 4, a, b)


def unpack_rows(packed):
    low = iota((8, 128), 0) < 4
    turned = pltpu.roll(packed, 4, 0)
    return jnp.where(low, packed, turned), jnp.where(low, turned, packed)


def fold(x):
    lane = iota((8, 128), 1)
    low, early = lane < 80, (lane & 7) < 4
    first = jnp.where(early, x[0:8], pltpu.roll(x[8:16], 4, 1))
    second = jnp.where(early, pltpu.roll(x[16:24], 80, 1), pltpu.roll(x[16:24], 36, 1))
    return jnp.where(low, first, second)


def unfold(x):
    lane = iota((8, 128), 1)
    third = jnp.where(lane < 48, pltpu.roll(x, 48, 1), pltpu.roll(x, 92, 1))
    return jnp.concatenate([x, pltpu.roll(x, 124, 1), third], axis=0)


def pack_kernel(*refs):
    sources, out, begin, held, sems = refs[:7], refs[7], refs[8], refs[9:16], refs[16]
    loads = [pltpu.make_async_copy(s, h, sems.at[i]) for i, (s, h) in enumerate(zip(sources, held))]
    for copy in loads:
        copy.start()
    for copy in loads[1:]:
        copy.wait()
    state, shift, coefs = held[0], held[1], held[2:]
    rows = state.shape[1]
    group = iota((rows, 128), 1) // 8
    edges = jnp.zeros((rows, 128), F32)
    for i, ref in enumerate(coefs):
        for l in range(2):
            a = 2 * i + l
            edges = jnp.where(group == a, pltpu.roll(ref[l].astype(F32), 8 * a + 4, 1), edges)
    eye = iota((rows, rows), 0) == iota((rows, rows), 1)
    for l in range(2):
        line = jnp.broadcast_to(shift[l : l + 1, :].astype(F32), (rows, rows))
        moved = jnp.sum(jnp.where(eye, line, 0.0), axis=1, keepdims=True).astype(I32)
        begin[l] = jnp.broadcast_to((-moved - 7) & 2047, (rows, 128))
    loads[0].wait()
    for fl in range(8):
        out[fl] = state[fl]
    out[8] = edges


def windows(circle, begin, l, at, target, fields):
    me = lax.axis_index("lon")
    first = begin[l, at : at + 8]
    spot = (first & 127) + iota((8, 128), 1)
    index, inside = spot & 127, spot < 128
    sector = ((me ^ target) + (first >> 7) - (me & 2)) & 15
    for fl in fields:
        block = [jnp.zeros((8, 128), F32) for _ in range(3)]
        for y in range(4):
            for c in range(2):
                value = circle[2 * y + c, fl, at : at + 8]
                for k in range(3):
                    block[k] = jnp.where(sector == ((4 * y + c - k) & 15), value, block[k])
        r = [jnp.take_along_axis(v, index, axis=1) for v in block]
        yield fl, jnp.where(inside, r[0], r[1]), jnp.where(inside, r[1], r[2])


def window_kernel(target, circle, begin, out):
    rows = circle.shape[2]
    me = lax.axis_index("lon")
    core = me & 1
    slot = iota((8, 128), 1) // 16
    for at in range(0, rows, 8):
        tails = jnp.zeros((8, 128), F32)
        for l in range(2):
            for fl, head, tail in windows(circle, begin, l, at, target, range(l, 8, 2)):
                out[rows * fl + at : rows * fl + at + 8] = head
                tails = jnp.where(slot == fl, pltpu.roll(tail, 16 * fl, 1) if fl else tail, tails)
        out[8 * rows + at : 8 * rows + at + 8] = tails
    if target == 0:
        out[9 * rows : 10 * rows] = circle[me // 4 * 2 + 1 - core, 8]
    else:
        outer = ((me ^ 2) + jnp.where(core == 0, 15, 1)) & 15
        outer = circle[outer // 4 * 2 + 1 - core, 8]
        outer = jnp.where(core == 0, outer, pltpu.roll(outer, 124, 1))
        out[9 * rows : 9 * rows + 8] = fold(outer)


def zonal_kernel(keep, swapped, zc, zf, mc, mf, cp, out, ea, eb):
    rows = zc.shape[1]
    me, band = lax.axis_index("lon"), lax.axis_index("lat")
    core = me & 1
    across = 1 - ((me >> 1) & 1)
    lane = iota((rows, 128), 1)
    outer = unfold(swapped[across, 9 * rows : 9 * rows + 8])
    outer = jnp.where(core == 0, outer, pltpu.roll(outer, 4, 1))
    early = jnp.where((lane & 7) < 4, 0, 1)
    beside = jnp.where(early == core, outer, keep[9 * rows : 10 * rows])

    def both(plane):
        at = plane * rows
        return keep[at : at + rows] + swapped[across, at : at + rows]

    def extended(ref, i, l):
        a = 2 * i + l
        own = pltpu.roll(ref[l].astype(F32), 4, 1)
        side = pltpu.roll(beside, 128 - 8 * a, 1) if a else beside
        return jnp.where(lane < 4, side, own), jnp.where(lane < 4, own, side)

    ends = both(8)
    slot = lane // 8
    tails = jnp.zeros((rows, 128), F32)
    for l in range(2):
        cells, frac = extended(zc, 0, l), extended(zf, 1, l)
        near, far = [offset_weights(frac[n], cells[n], -2, 2) for n in range(2)]
        for f in range(4):
            fl = 2 * f + l
            end = pltpu.roll(ends, 128 - 16 * fl, 1) if fl else ends
            head = both(fl)
            total, tail = near[0] * head, far[0] * end
            for d in range(1, 8):
                moved = pltpu.roll(end, 128 - d, 1)
                shifted = jnp.where(lane < 128 - d, pltpu.roll(head, 128 - d, 1), moved)
                total = total + near[d] * shifted
                tail = tail + far[d] * moved
            out[fl] = total
            tail = pltpu.roll(tail, 8 * fl, 1) if fl else tail
            tails = jnp.where(slot == fl, tail, tails)
    for i, ref in enumerate((mc, mf, cp)):
        for l in range(2):
            a = 8 + 2 * i + l
            out[a + 1], tail = extended(ref, i + 2, l)
            tails = jnp.where(slot == a, pltpu.roll(tail, 8 * a, 1), tails)
    out[8] = tails

    even = (band & 1) == 0
    for e, top in ((ea, jnp.logical_not(even)), (eb, even)):
        take = pl.ds(pl.multiple_of(jnp.where(top, 0, rows - 8), 8), 8)
        for plane in range(9):
            e[plane] = out[plane, take]
        for i in range(3):
            e[9 + i] = pack_rows(out[9 + 2 * i, take], out[10 + 2 * i, take], top)


def sweep_kernel(main, ga, gb, result, done, sems):
    rows = main.shape[1]
    total = rows + 8
    band, bands = lax.axis_index("lat"), lax.axis_size("lat")
    even = (band & 1) == 0
    lane, row = iota((total, 128), 1), iota((total, 128), 0)
    outside = ((row < 4) & (band == 0)) | ((row >= rows + 4) & (band == bands - 1))
    tall = iota((rows + 16, 128), 0)
    beyond = ((tall < 8) & (band == 0)) | ((tall >= rows + 8) & (band == bands - 1))

    def pick(plane):
        above = jnp.where(even, gb[plane], ga[0, plane])
        below = jnp.where(even, ga[1, plane], gb[plane])
        return above, below

    def joined(ends, own):
        return jnp.concatenate([ends[0], own, ends[1]], axis=0)

    def rotated(x, lanes):
        return pltpu.roll(x, lanes % 128, 1) if lanes % 128 else x

    def prepare(cells, frac, coupling):
        weights = offset_weights(frac, cells, -1, 1)
        inverse = jnp.where(outside, 0.0, 1.0 / (1.0 + 4.0 * coupling))
        return weights, inverse, coupling * inverse

    def source_of(value, weights):
        value = jnp.where(beyond, 0.0, value)
        source = jnp.zeros((total, 128), F32)
        for i in range(6):
            moved = pltpu.roll(value, rows + 16 - (2 + i), 0)[:total]
            source = source + weights[i] * moved
        return jnp.where(outside, 0.0, source)

    packs = [[unpack_rows(v) for v in pick(9 + i)] for i in range(3)]
    tails = joined(pick(8), main[8])
    edge = pltpu.roll(tails, rows + 12, 0)[:total]
    group = []
    for i in range(3):
        v = rotated(edge, 64 - 16 * i)
        v = jnp.where(lane < 16, v, pltpu.roll(v, 16, 1))
        group.append(jnp.where(lane < 32, v, pltpu.roll(v, 32, 1)))
    weights, inverse, tail_factor = prepare(*group)
    tail = source_of(tails, weights)
    tail_source = tail * inverse
    phi, source, factor = [None] * 8, [None] * 8, [None] * 8
    for l in range(2):
        coefs = []
        for i in range(3):
            own = joined([v[l] for v in packs[i]], main[9 + 2 * i + l])
            coefs.append(pltpu.roll(own, rows + 12, 0)[:total])
        weights, inverse, level_factor = prepare(*coefs)
        for f in range(4):
            fl = 2 * f + l
            value = source_of(joined(pick(fl), main[fl]), weights)
            phi[fl] = rotated(value, 8 * fl)
            source[fl] = rotated(value * inverse, 8 * fl)
            factor[fl] = rotated(level_factor, 8 * fl)
    for sweep in range(SWEEPS):
        old_tail = tail
        tail_left, tail_right = pltpu.roll(tail, 1, 1), pltpu.roll(tail, 127, 1)
        for fl in range(8):
            old = phi[fl]
            left = pltpu.roll(old, 1, 1)
            tail_left = jnp.where(lane == 8 * fl, left, tail_left)
            right = jnp.where(lane == (8 * fl - 1) % 128, tail_right, pltpu.roll(old, 127, 1))
            beside = pltpu.roll(old, 1, 0) + pltpu.roll(old, total - 1, 0) + left + right
            phi[fl] = source[fl] + factor[fl] * beside
        beside = pltpu.roll(old_tail, 1, 0) + pltpu.roll(old_tail, total - 1, 0)
        tail = tail_source + tail_factor * (beside + tail_left + tail_right)
    copies = []
    for fl in range(8):
        whole = jnp.where((lane >= 8 * fl) & (lane < 8 * fl + 4), tail, phi[fl])
        whole = rotated(whole, -4 - 8 * fl)
        done[fl] = pltpu.roll(whole, total - 4, 0)[:rows]
        copies.append(pltpu.make_async_copy(done.at[fl], result.at[fl], sems.at[fl]))
        copies[-1].start()
    for copy in copies:
        copy.wait()


def call(kernel, shapes, limit=32, **more):
    return pl.pallas_call(
        kernel,
        out_shape=[jax.ShapeDtypeStruct(s, d) for s, d in shapes],
        compiler_params=pltpu.CompilerParams(vmem_limit_bytes=limit << 20),
        **more,
    )


def body(state, zonal_shift, zonal_cells, zonal_fraction, merid_cells, merid_fraction, coupling):
    rows = state.shape[2]
    bands = lax.axis_size("lat")
    coefs = (zonal_cells, zonal_fraction, merid_cells, merid_fraction, coupling)
    loads = (state.reshape(8, rows, 128), zonal_shift, *coefs)
    lat_pairs = [
        [i * SECTORS + s, (i + 1) * SECTORS + s] for i in range(0, bands, 2) for s in range(SECTORS)
    ]
    lat_swaps = [p for i in range(1, bands - 1, 2) for p in ((i, i + 1), (i + 1, i))]

    hbm = pl.BlockSpec(memory_space=pltpu.HBM)
    packed, begin = call(
        pack_kernel,
        [((9, rows, 128), F32), ((2, rows, 128), I32)],
        60,
        scratch_shapes=[pltpu.VMEM(v.shape, v.dtype) for v in loads]
        + [pltpu.SemaphoreType.DMA((7,))],
        in_specs=[hbm] * 7,
    )(*loads)
    circle = lax.all_gather(packed, "lon", axis_index_groups=SIDES)
    (send,) = call(partial(window_kernel, 2), [((9 * rows + 8, 128), F32)])(circle, begin)
    (keep,) = call(partial(window_kernel, 0), [((10 * rows, 128), F32)])(circle, begin)
    swapped = lax.all_gather(send, "lon", axis_index_groups=Z_PAIRS)
    main, ea, eb = call(
        zonal_kernel, [((15, rows, 128), F32), ((12, 8, 128), F32), ((12, 8, 128), F32)]
    )(keep, swapped, *coefs)
    gb = lax.ppermute(eb, "lat", lat_swaps)
    ga = lax.all_gather(ea, ("lat", "lon"), axis_index_groups=lat_pairs)
    (advanced,) = call(
        sweep_kernel,
        [((8, rows, 128), F32)],
        scratch_shapes=[pltpu.VMEM((8, rows, 128), F32), pltpu.SemaphoreType.DMA((8,))],
        out_specs=[hbm],
    )(main, ga, gb)
    return advanced.reshape(state.shape)


def solution(mesh):
    in_specs = (
        P(None, None, "lat", "lon"),
        P(None, "lat"),
        P(None, "lat", "lon"),
        P(None, "lat", "lon"),
        P(None, "lat", "lon"),
        P(None, "lat", "lon"),
        P(None, "lat", "lon"),
    )
    out_specs = P(None, None, "lat", "lon")
    return jax.shard_map(body, mesh=mesh, in_specs=in_specs, out_specs=out_specs, check_vma=False)
```

```python
from functools import partial

import jax
import jax.numpy as jnp
from jax import lax
from jax.experimental import pallas as pl
from jax.experimental.pallas import tpu as pltpu
from jax.sharding import PartitionSpec as P

SWEEPS = 4
F32 = jnp.float32
I32 = jnp.int32
SECTORS = 16
Z_PAIRS = [[4 * y + c, 4 * y + 2 + c] for y in range(4) for c in range(2)]
SIDES = [[4 * y + 2 * z + c for y in range(4) for c in range(2)] for z in range(2)]


def iota(shape, dim):
    return lax.broadcasted_iota(I32, shape, dim)


def cubic_weights(frac):
    return (
        -frac * (frac - 1.0) * (frac - 2.0) / 6.0,
        (frac + 1.0) * (frac - 1.0) * (frac - 2.0) / 2.0,
        -(frac + 1.0) * frac * (frac - 2.0) / 2.0,
        (frac + 1.0) * frac * (frac - 1.0) / 6.0,
    )


def offset_weights(frac, cells, lowest, highest):
    w = cubic_weights(frac)
    result = []
    for offset in range(-1 - highest, 3 - lowest):
        total = jnp.zeros_like(frac)
        for k in range(4):
            c = k - 1 - offset
            if lowest <= c <= highest:
                total = jnp.where(cells == float(c), w[k], total)
        result.append(total)
    return result


def pack_rows(first, second, top):
    a = jnp.where(top, first, pltpu.roll(first, 4, 0))
    b = jnp.where(top, pltpu.roll(second, 4, 0), second)
    return jnp.where(iota((8, 128), 0) < 4, a, b)


def unpack_rows(packed):
    low = iota((8, 128), 0) < 4
    turned = pltpu.roll(packed, 4, 0)
    return jnp.where(low, packed, turned), jnp.where(low, turned, packed)


def fold(x):
    lane = iota((8, 128), 1)
    low, early = lane < 80, (lane & 7) < 4
    first = jnp.where(early, x[0:8], pltpu.roll(x[8:16], 4, 1))
    second = jnp.where(early, pltpu.roll(x[16:24], 80, 1), pltpu.roll(x[16:24], 36, 1))
    return jnp.where(low, first, second)


def unfold(x):
    lane = iota((8, 128), 1)
    third = jnp.where(lane < 48, pltpu.roll(x, 48, 1), pltpu.roll(x, 92, 1))
    return jnp.concatenate([x, pltpu.roll(x, 124, 1), third], axis=0)


def pack_kernel(*refs):
    sources, out, begin, held, sems = refs[:7], refs[7], refs[8], refs[9:16], refs[16]
    loads = [pltpu.make_async_copy(s, h, sems.at[i]) for i, (s, h) in enumerate(zip(sources, held))]
    for copy in loads:
        copy.start()
    for copy in loads[1:]:
        copy.wait()
    state, shift, coefs = held[0], held[1], held[2:]
    rows = state.shape[1]
    group = iota((rows, 128), 1) // 8
    edges = jnp.zeros((rows, 128), F32)
    for i, ref in enumerate(coefs):
        for l in range(2):
            a = 2 * i + l
            edges = jnp.where(group == a, pltpu.roll(ref[l].astype(F32), 8 * a + 4, 1), edges)
    eye = iota((rows, rows), 0) == iota((rows, rows), 1)
    for l in range(2):
        line = jnp.broadcast_to(shift[l : l + 1, :].astype(F32), (rows, rows))
        moved = jnp.sum(jnp.where(eye, line, 0.0), axis=1, keepdims=True).astype(I32)
        begin[l] = jnp.broadcast_to((-moved - 7) & 2047, (rows, 128))
    loads[0].wait()
    for fl in range(8):
        out[fl] = state[fl]
    out[8] = edges


def windows(circle, begin, l, at, target, fields):
    me = lax.axis_index("lon")
    first = begin[l, at : at + 8]
    spot = (first & 127) + iota((8, 128), 1)
    index, inside = spot & 127, spot < 128
    sector = ((me ^ target) + (first >> 7) - (me & 2)) & 15
    for fl in fields:
        block = [jnp.zeros((8, 128), F32) for _ in range(3)]
        for y in range(4):
            for c in range(2):
                value = circle[2 * y + c, fl, at : at + 8]
                for k in range(3):
                    block[k] = jnp.where(sector == ((4 * y + c - k) & 15), value, block[k])
        r = [jnp.take_along_axis(v, index, axis=1) for v in block]
        yield fl, jnp.where(inside, r[0], r[1]), jnp.where(inside, r[1], r[2])


def window_kernel(target, circle, begin, out):
    rows = circle.shape[2]
    me = lax.axis_index("lon")
    core = me & 1
    slot = iota((8, 128), 1) // 16
    for at in range(0, rows, 8):
        tails = jnp.zeros((8, 128), F32)
        for l in range(2):
            for fl, head, tail in windows(circle, begin, l, at, target, range(l, 8, 2)):
                out[rows * fl + at : rows * fl + at + 8] = head
                tails = jnp.where(slot == fl, pltpu.roll(tail, 16 * fl, 1) if fl else tail, tails)
        out[8 * rows + at : 8 * rows + at + 8] = tails
    if target == 0:
        out[9 * rows : 10 * rows] = circle[me // 4 * 2 + 1 - core, 8]
    else:
        outer = ((me ^ 2) + jnp.where(core == 0, 15, 1)) & 15
        outer = circle[outer // 4 * 2 + 1 - core, 8]
        outer = jnp.where(core == 0, outer, pltpu.roll(outer, 124, 1))
        out[9 * rows : 9 * rows + 8] = fold(outer)


def zonal_kernel(keep, swapped, zc, zf, mc, mf, cp, out, ea, eb):
    rows = zc.shape[1]
    me, band = lax.axis_index("lon"), lax.axis_index("lat")
    core = me & 1
    across = 1 - ((me >> 1) & 1)
    lane = iota((rows, 128), 1)
    outer = unfold(swapped[across, 9 * rows : 9 * rows + 8])
    outer = jnp.where(core == 0, outer, pltpu.roll(outer, 4, 1))
    early = jnp.where((lane & 7) < 4, 0, 1)
    beside = jnp.where(early == core, outer, keep[9 * rows : 10 * rows])

    def both(plane):
        at = plane * rows
        return keep[at : at + rows] + swapped[across, at : at + rows]

    def extended(ref, i, l):
        a = 2 * i + l
        own = pltpu.roll(ref[l].astype(F32), 4, 1)
        side = pltpu.roll(beside, 128 - 8 * a, 1) if a else beside
        return jnp.where(lane < 4, side, own), jnp.where(lane < 4, own, side)

    ends = both(8)
    slot = lane // 8
    tails = jnp.zeros((rows, 128), F32)
    for l in range(2):
        cells, frac = extended(zc, 0, l), extended(zf, 1, l)
        near, far = [offset_weights(frac[n], cells[n], -2, 2) for n in range(2)]
        for f in range(4):
            fl = 2 * f + l
            end = pltpu.roll(ends, 128 - 16 * fl, 1) if fl else ends
            head = both(fl)
            total, tail = near[0] * head, far[0] * end
            for d in range(1, 8):
                moved = pltpu.roll(end, 128 - d, 1)
                shifted = jnp.where(lane < 128 - d, pltpu.roll(head, 128 - d, 1), moved)
                total = total + near[d] * shifted
                tail = tail + far[d] * moved
            out[fl] = total
            tail = pltpu.roll(tail, 8 * fl, 1) if fl else tail
            tails = jnp.where(slot == fl, tail, tails)
    for i, ref in enumerate((mc, mf, cp)):
        for l in range(2):
            a = 8 + 2 * i + l
            out[a + 1], tail = extended(ref, i + 2, l)
            tails = jnp.where(slot == a, pltpu.roll(tail, 8 * a, 1), tails)
    out[8] = tails

    even = (band & 1) == 0
    for e, top in ((ea, jnp.logical_not(even)), (eb, even)):
        take = pl.ds(pl.multiple_of(jnp.where(top, 0, rows - 8), 8), 8)
        for plane in range(9):
            e[plane] = out[plane, take]
        for i in range(3):
            e[9 + i] = pack_rows(out[9 + 2 * i, take], out[10 + 2 * i, take], top)


def sweep_kernel(main, ga, gb, result, done, sems):
    rows = main.shape[1]
    total = rows + 8
    band, bands = lax.axis_index("lat"), lax.axis_size("lat")
    even = (band & 1) == 0
    lane, row = iota((total, 128), 1), iota((total, 128), 0)
    outside = ((row < 4) & (band == 0)) | ((row >= rows + 4) & (band == bands - 1))
    tall = iota((rows + 16, 128), 0)
    beyond = ((tall < 8) & (band == 0)) | ((tall >= rows + 8) & (band == bands - 1))

    def pick(plane):
        above = jnp.where(even, gb[plane], ga[0, plane])
        below = jnp.where(even, ga[1, plane], gb[plane])
        return above, below

    def joined(ends, own):
        return jnp.concatenate([ends[0], own, ends[1]], axis=0)

    def rotated(x, lanes):
        return pltpu.roll(x, lanes % 128, 1) if lanes % 128 else x

    def prepare(cells, frac, coupling):
        weights = offset_weights(frac, cells, -1, 1)
        inverse = jnp.where(outside, 0.0, 1.0 / (1.0 + 4.0 * coupling))
        return weights, inverse, coupling * inverse

    def source_of(value, weights):
        value = jnp.where(beyond, 0.0, value)
        source = jnp.zeros((total, 128), F32)
        for i in range(6):
            moved = pltpu.roll(value, rows + 16 - (2 + i), 0)[:total]
            source = source + weights[i] * moved
        return jnp.where(outside, 0.0, source)

    packs = [[unpack_rows(v) for v in pick(9 + i)] for i in range(3)]
    tails = joined(pick(8), main[8])
    edge = pltpu.roll(tails, rows + 12, 0)[:total]
    group = []
    for i in range(3):
        v = rotated(edge, 64 - 16 * i)
        v = jnp.where(lane < 16, v, pltpu.roll(v, 16, 1))
        group.append(jnp.where(lane < 32, v, pltpu.roll(v, 32, 1)))
    weights, inverse, tail_factor = prepare(*group)
    tail = source_of(tails, weights)
    tail_source = tail * inverse
    phi, source, factor = [None] * 8, [None] * 8, [None] * 8
    for l in range(2):
        coefs = []
        for i in range(3):
            own = joined([v[l] for v in packs[i]], main[9 + 2 * i + l])
            coefs.append(pltpu.roll(own, rows + 12, 0)[:total])
        weights, inverse, level_factor = prepare(*coefs)
        for f in range(4):
            fl = 2 * f + l
            value = source_of(joined(pick(fl), main[fl]), weights)
            phi[fl] = rotated(value, 8 * fl)
            source[fl] = rotated(value * inverse, 8 * fl)
            factor[fl] = rotated(level_factor, 8 * fl)
    for sweep in range(SWEEPS):
        old_tail = tail
        tail_left, tail_right = pltpu.roll(tail, 1, 1), pltpu.roll(tail, 127, 1)
        for fl in range(8):
            old = phi[fl]
            left = pltpu.roll(old, 1, 1)
            tail_left = jnp.where(lane == 8 * fl, left, tail_left)
            right = jnp.where(lane == (8 * fl - 1) % 128, tail_right, pltpu.roll(old, 127, 1))
            beside = pltpu.roll(old, 1, 0) + pltpu.roll(old, total - 1, 0) + left + right
            phi[fl] = source[fl] + factor[fl] * beside
        beside = pltpu.roll(old_tail, 1, 0) + pltpu.roll(old_tail, total - 1, 0)
        tail = tail_source + tail_factor * (beside + tail_left + tail_right)
    copies = []
    for fl in range(8):
        whole = jnp.where((lane >= 8 * fl) & (lane < 8 * fl + 4), tail, phi[fl])
        whole = rotated(whole, -4 - 8 * fl)
        done[fl] = pltpu.roll(whole, total - 4, 0)[:rows]
        copies.append(pltpu.make_async_copy(done.at[fl], result.at[fl], sems.at[fl]))
        copies[-1].start()
    for copy in copies:
        copy.wait()


def call(kernel, shapes, limit=32, **more):
    return pl.pallas_call(
        kernel,
        out_shape=[jax.ShapeDtypeStruct(s, d) for s, d in shapes],
        compiler_params=pltpu.CompilerParams(vmem_limit_bytes=limit << 20),
        **more,
    )


def body(state, zonal_shift, zonal_cells, zonal_fraction, merid_cells, merid_fraction, coupling):
    rows = state.shape[2]
    bands = lax.axis_size("lat")
    coefs = (zonal_cells, zonal_fraction, merid_cells, merid_fraction, coupling)
    loads = (state.reshape(8, rows, 128), zonal_shift, *coefs)
    lat_pairs = [
        [i * SECTORS + s, (i + 1) * SECTORS + s] for i in range(0, bands, 2) for s in range(SECTORS)
    ]
    lat_swaps = [p for i in range(1, bands - 1, 2) for p in ((i, i + 1), (i + 1, i))]

    hbm = pl.BlockSpec(memory_space=pltpu.HBM)
    packed, begin = call(
        pack_kernel,
        [((9, rows, 128), F32), ((2, rows, 128), I32)],
        32,
        scratch_shapes=[pltpu.VMEM(v.shape, v.dtype) for v in loads]
        + [pltpu.SemaphoreType.DMA((7,))],
        in_specs=[hbm] * 7,
    )(*[pltpu.with_memory_space_constraint(v, pltpu.HBM) for v in loads])
    circle = lax.all_gather(packed, "lon", axis_index_groups=SIDES)
    (send,) = call(partial(window_kernel, 2), [((9 * rows + 8, 128), F32)])(circle, begin)
    (keep,) = call(partial(window_kernel, 0), [((10 * rows, 128), F32)])(circle, begin)
    swapped = lax.all_gather(send, "lon", axis_index_groups=Z_PAIRS)
    main, ea, eb = call(
        zonal_kernel, [((15, rows, 128), F32), ((12, 8, 128), F32), ((12, 8, 128), F32)]
    )(keep, swapped, *coefs)
    gb = lax.ppermute(eb, "lat", lat_swaps)
    ga = lax.all_gather(ea, ("lat", "lon"), axis_index_groups=lat_pairs)
    (advanced,) = call(
        sweep_kernel,
        [((8, rows, 128), F32)],
        scratch_shapes=[pltpu.VMEM((8, rows, 128), F32), pltpu.SemaphoreType.DMA((8,))],
        out_specs=[hbm],
    )(main, ga, gb)
    return advanced.reshape(state.shape)


def solution(mesh):
    in_specs = (
        P(None, None, "lat", "lon"),
        P(None, "lat"),
        P(None, "lat", "lon"),
        P(None, "lat", "lon"),
        P(None, "lat", "lon"),
        P(None, "lat", "lon"),
        P(None, "lat", "lon"),
    )
    out_specs = P(None, None, "lat", "lon")
    return jax.shard_map(body, mesh=mesh, in_specs=in_specs, out_specs=out_specs, check_vma=False)
```

```python
from functools import partial

import jax
import jax.numpy as jnp
from jax import lax
from jax.experimental import pallas as pl
from jax.experimental.pallas import tpu as pltpu
from jax.sharding import PartitionSpec as P

SWEEPS = 4
F32 = jnp.float32
I32 = jnp.int32
SECTORS = 16
Z_PAIRS = [[4 * y + c, 4 * y + 2 + c] for y in range(4) for c in range(2)]
SIDES = [[4 * y + 2 * z + c for y in range(4) for c in range(2)] for z in range(2)]


def iota(shape, dim):
    return lax.broadcasted_iota(I32, shape, dim)


def cubic_weights(frac):
    return (
        -frac * (frac - 1.0) * (frac - 2.0) / 6.0,
        (frac + 1.0) * (frac - 1.0) * (frac - 2.0) / 2.0,
        -(frac + 1.0) * frac * (frac - 2.0) / 2.0,
        (frac + 1.0) * frac * (frac - 1.0) / 6.0,
    )


def offset_weights(frac, cells, lowest, highest):
    w = cubic_weights(frac)
    result = []
    for offset in range(-1 - highest, 3 - lowest):
        total = jnp.zeros_like(frac)
        for k in range(4):
            c = k - 1 - offset
            if lowest <= c <= highest:
                total = jnp.where(cells == float(c), w[k], total)
        result.append(total)
    return result


def pack_rows(first, second, top):
    a = jnp.where(top, first, pltpu.roll(first, 4, 0))
    b = jnp.where(top, pltpu.roll(second, 4, 0), second)
    return jnp.where(iota((8, 128), 0) < 4, a, b)


def unpack_rows(packed):
    low = iota((8, 128), 0) < 4
    turned = pltpu.roll(packed, 4, 0)
    return jnp.where(low, packed, turned), jnp.where(low, turned, packed)


def fold(x):
    lane = iota((8, 128), 1)
    low, early = lane < 80, (lane & 7) < 4
    first = jnp.where(early, x[0:8], pltpu.roll(x[8:16], 4, 1))
    second = jnp.where(early, pltpu.roll(x[16:24], 80, 1), pltpu.roll(x[16:24], 36, 1))
    return jnp.where(low, first, second)


def unfold(x):
    lane = iota((8, 128), 1)
    third = jnp.where(lane < 48, pltpu.roll(x, 48, 1), pltpu.roll(x, 92, 1))
    return jnp.concatenate([x, pltpu.roll(x, 124, 1), third], axis=0)


def pack_kernel(*refs):
    sources, out, begin, held, sems = refs[:7], refs[7], refs[8], refs[9:16], refs[16]
    loads = [pltpu.make_async_copy(s, h, sems.at[i]) for i, (s, h) in enumerate(zip(sources, held))]
    for copy in loads:
        copy.start()
    for copy in loads[1:]:
        copy.wait()
    state, shift, coefs = held[0], held[1], held[2:]
    rows = state.shape[1]
    group = iota((rows, 128), 1) // 8
    edges = jnp.zeros((rows, 128), F32)
    for i, ref in enumerate(coefs):
        for l in range(2):
            a = 2 * i + l
            edges = jnp.where(group == a, pltpu.roll(ref[l].astype(F32), 8 * a + 4, 1), edges)
    eye = iota((rows, rows), 0) == iota((rows, rows), 1)
    for l in range(2):
        line = jnp.broadcast_to(shift[l : l + 1, :].astype(F32), (rows, rows))
        moved = jnp.sum(jnp.where(eye, line, 0.0), axis=1, keepdims=True).astype(I32)
        begin[l] = jnp.broadcast_to((-moved - 7) & 2047, (rows, 128))
    loads[0].wait()
    for fl in range(8):
        out[fl] = state[fl]
    out[8] = edges


def windows(circle, begin, l, at, target, fields):
    me = lax.axis_index("lon")
    first = begin[l, at : at + 8]
    spot = (first & 127) + iota((8, 128), 1)
    index, inside = spot & 127, spot < 128
    sector = ((me ^ target) + (first >> 7) - (me & 2)) & 15
    for fl in fields:
        block = [jnp.zeros((8, 128), F32) for _ in range(3)]
        for y in range(4):
            for c in range(2):
                value = circle[2 * y + c, fl, at : at + 8]
                for k in range(3):
                    block[k] = jnp.where(sector == ((4 * y + c - k) & 15), value, block[k])
        r = [jnp.take_along_axis(v, index, axis=1) for v in block]
        yield fl, jnp.where(inside, r[0], r[1]), jnp.where(inside, r[1], r[2])


def window_kernel(target, circle, begin, out):
    rows = circle.shape[2]
    me = lax.axis_index("lon")
    core = me & 1
    slot = iota((8, 128), 1) // 16
    for at in range(0, rows, 8):
        tails = jnp.zeros((8, 128), F32)
        for l in range(2):
            for fl, head, tail in windows(circle, begin, l, at, target, range(l, 8, 2)):
                out[rows * fl + at : rows * fl + at + 8] = head
                tails = jnp.where(slot == fl, pltpu.roll(tail, 16 * fl, 1) if fl else tail, tails)
        out[8 * rows + at : 8 * rows + at + 8] = tails
    if target == 0:
        out[9 * rows : 10 * rows] = circle[me // 4 * 2 + 1 - core, 8]
    else:
        outer = ((me ^ 2) + jnp.where(core == 0, 15, 1)) & 15
        outer = circle[outer // 4 * 2 + 1 - core, 8]
        outer = jnp.where(core == 0, outer, pltpu.roll(outer, 124, 1))
        out[9 * rows : 9 * rows + 8] = fold(outer)


def zonal_kernel(keep, swapped, zc, zf, mc, mf, cp, out, ea, eb):
    rows = zc.shape[1]
    me, band = lax.axis_index("lon"), lax.axis_index("lat")
    core = me & 1
    across = 1 - ((me >> 1) & 1)
    lane = iota((rows, 128), 1)
    outer = unfold(swapped[across, 9 * rows : 9 * rows + 8])
    outer = jnp.where(core == 0, outer, pltpu.roll(outer, 4, 1))
    early = jnp.where((lane & 7) < 4, 0, 1)
    beside = jnp.where(early == core, outer, keep[9 * rows : 10 * rows])

    def both(plane):
        at = plane * rows
        return keep[at : at + rows] + swapped[across, at : at + rows]

    def extended(ref, i, l):
        a = 2 * i + l
        own = pltpu.roll(ref[l].astype(F32), 4, 1)
        side = pltpu.roll(beside, 128 - 8 * a, 1) if a else beside
        return jnp.where(lane < 4, side, own), jnp.where(lane < 4, own, side)

    ends = both(8)
    slot = lane // 8
    tails = jnp.zeros((rows, 128), F32)
    for l in range(2):
        cells, frac = extended(zc, 0, l), extended(zf, 1, l)
        near, far = [offset_weights(frac[n], cells[n], -2, 2) for n in range(2)]
        fields = range(l, 8, 2)
        heads = {fl: both(fl) for fl in fields}
        rests = {fl: pltpu.roll(ends, 128 - 16 * fl, 1) if fl else ends for fl in fields}
        total = {fl: near[0] * heads[fl] for fl in fields}
        tail = {fl: far[0] * rests[fl] for fl in fields}
        for d in range(1, 8):
            for fl in fields:
                moved = pltpu.roll(rests[fl], 128 - d, 1)
                shifted = jnp.where(lane < 128 - d, pltpu.roll(heads[fl], 128 - d, 1), moved)
                total[fl] = total[fl] + near[d] * shifted
                tail[fl] = tail[fl] + far[d] * moved
        for fl in fields:
            out[fl] = total[fl]
            end = pltpu.roll(tail[fl], 8 * fl, 1) if fl else tail[fl]
            tails = jnp.where(slot == fl, end, tails)
    for i, ref in enumerate((mc, mf, cp)):
        for l in range(2):
            a = 8 + 2 * i + l
            out[a + 1], tail = extended(ref, i + 2, l)
            tails = jnp.where(slot == a, pltpu.roll(tail, 8 * a, 1), tails)
    out[8] = tails

    even = (band & 1) == 0
    for e, top in ((ea, jnp.logical_not(even)), (eb, even)):
        take = pl.ds(pl.multiple_of(jnp.where(top, 0, rows - 8), 8), 8)
        for plane in range(9):
            e[plane] = out[plane, take]
        for i in range(3):
            e[9 + i] = pack_rows(out[9 + 2 * i, take], out[10 + 2 * i, take], top)


def sweep_kernel(main, ga, gb, result, done, sems):
    rows = main.shape[1]
    total = rows + 8
    band, bands = lax.axis_index("lat"), lax.axis_size("lat")
    even = (band & 1) == 0
    lane, row = iota((total, 128), 1), iota((total, 128), 0)
    outside = ((row < 4) & (band == 0)) | ((row >= rows + 4) & (band == bands - 1))
    tall = iota((rows + 16, 128), 0)
    beyond = ((tall < 8) & (band == 0)) | ((tall >= rows + 8) & (band == bands - 1))

    def pick(plane):
        above = jnp.where(even, gb[plane], ga[0, plane])
        below = jnp.where(even, ga[1, plane], gb[plane])
        return above, below

    def joined(ends, own):
        return jnp.concatenate([ends[0], own, ends[1]], axis=0)

    def rotated(x, lanes):
        return pltpu.roll(x, lanes % 128, 1) if lanes % 128 else x

    def prepare(cells, frac, coupling):
        weights = offset_weights(frac, cells, -1, 1)
        inverse = jnp.where(outside, 0.0, 1.0 / (1.0 + 4.0 * coupling))
        return weights, inverse, coupling * inverse

    def source_of(values, weights):
        values = [jnp.where(beyond, 0.0, v) for v in values]
        sources = [jnp.zeros((total, 128), F32) for _ in values]
        for i in range(6):
            for n, value in enumerate(values):
                moved = pltpu.roll(value, rows + 16 - (2 + i), 0)[:total]
                sources[n] = sources[n] + weights[i] * moved
        return [jnp.where(outside, 0.0, v) for v in sources]

    packs = [[unpack_rows(v) for v in pick(9 + i)] for i in range(3)]
    tails = joined(pick(8), main[8])
    edge = pltpu.roll(tails, rows + 12, 0)[:total]
    group = []
    for i in range(3):
        v = rotated(edge, 64 - 16 * i)
        v = jnp.where(lane < 16, v, pltpu.roll(v, 16, 1))
        group.append(jnp.where(lane < 32, v, pltpu.roll(v, 32, 1)))
    weights, inverse, tail_factor = prepare(*group)
    (tail,) = source_of([tails], weights)
    tail_source = tail * inverse
    phi, source, factor = [None] * 8, [None] * 8, [None] * 8
    for l in range(2):
        coefs = []
        for i in range(3):
            own = joined([v[l] for v in packs[i]], main[9 + 2 * i + l])
            coefs.append(pltpu.roll(own, rows + 12, 0)[:total])
        weights, inverse, level_factor = prepare(*coefs)
        fields = range(l, 8, 2)
        values = source_of([joined(pick(fl), main[fl]) for fl in fields], weights)
        for fl, value in zip(fields, values):
            phi[fl] = rotated(value, 8 * fl)
            source[fl] = rotated(value * inverse, 8 * fl)
            factor[fl] = rotated(level_factor, 8 * fl)
    copies = []
    for sweep in range(SWEEPS):
        tail_left, tail_right = pltpu.roll(tail, 1, 1), pltpu.roll(tail, 127, 1)
        lefts = [pltpu.roll(v, 1, 1) for v in phi]
        for fl in range(8):
            tail_left = jnp.where(lane == 8 * fl, lefts[fl], tail_left)
        beside = pltpu.roll(tail, 1, 0) + pltpu.roll(tail, total - 1, 0)
        tail = tail_source + tail_factor * (beside + tail_left + tail_right)
        for fl in range(8):
            old = phi[fl]
            right = jnp.where(lane == (8 * fl - 1) % 128, tail_right, pltpu.roll(old, 127, 1))
            beside = pltpu.roll(old, 1, 0) + pltpu.roll(old, total - 1, 0) + lefts[fl] + right
            phi[fl] = source[fl] + factor[fl] * beside
            if sweep == SWEEPS - 1:
                whole = jnp.where((lane >= 8 * fl) & (lane < 8 * fl + 4), tail, phi[fl])
                whole = rotated(whole, -4 - 8 * fl)
                done[fl] = pltpu.roll(whole, total - 4, 0)[:rows]
                copies.append(pltpu.make_async_copy(done.at[fl], result.at[fl], sems.at[fl]))
                copies[-1].start()
    for copy in copies:
        copy.wait()


def call(kernel, shapes, limit=32, **more):
    return pl.pallas_call(
        kernel,
        out_shape=[jax.ShapeDtypeStruct(s, d) for s, d in shapes],
        compiler_params=pltpu.CompilerParams(vmem_limit_bytes=limit << 20),
        **more,
    )


def body(state, zonal_shift, zonal_cells, zonal_fraction, merid_cells, merid_fraction, coupling):
    rows = state.shape[2]
    bands = lax.axis_size("lat")
    coefs = (zonal_cells, zonal_fraction, merid_cells, merid_fraction, coupling)
    loads = (state.reshape(8, rows, 128), zonal_shift, *coefs)
    lat_pairs = [
        [i * SECTORS + s, (i + 1) * SECTORS + s] for i in range(0, bands, 2) for s in range(SECTORS)
    ]
    lat_swaps = [p for i in range(1, bands - 1, 2) for p in ((i, i + 1), (i + 1, i))]

    hbm = pl.BlockSpec(memory_space=pltpu.HBM)
    packed, begin = call(
        pack_kernel,
        [((9, rows, 128), F32), ((2, rows, 128), I32)],
        32,
        scratch_shapes=[pltpu.VMEM(v.shape, v.dtype) for v in loads]
        + [pltpu.SemaphoreType.DMA((7,))],
        in_specs=[hbm] * 7,
    )(*[pltpu.with_memory_space_constraint(v, pltpu.HBM) for v in loads])
    circle = lax.all_gather(packed, "lon", axis_index_groups=SIDES)
    (send,) = call(partial(window_kernel, 2), [((9 * rows + 8, 128), F32)])(circle, begin)
    (keep,) = call(partial(window_kernel, 0), [((10 * rows, 128), F32)])(circle, begin)
    swapped = lax.all_gather(send, "lon", axis_index_groups=Z_PAIRS)
    main, ea, eb = call(
        zonal_kernel, [((15, rows, 128), F32), ((12, 8, 128), F32), ((12, 8, 128), F32)]
    )(keep, swapped, *coefs)
    gb = lax.ppermute(eb, "lat", lat_swaps)
    ga = lax.all_gather(ea, ("lat", "lon"), axis_index_groups=lat_pairs)
    (advanced,) = call(
        sweep_kernel,
        [((8, rows, 128), F32)],
        scratch_shapes=[pltpu.VMEM((8, rows, 128), F32), pltpu.SemaphoreType.DMA((8,))],
        out_specs=[hbm],
    )(main, ga, gb)
    return advanced.reshape(state.shape)


def solution(mesh):
    in_specs = (
        P(None, None, "lat", "lon"),
        P(None, "lat"),
        P(None, "lat", "lon"),
        P(None, "lat", "lon"),
        P(None, "lat", "lon"),
        P(None, "lat", "lon"),
        P(None, "lat", "lon"),
    )
    out_specs = P(None, None, "lat", "lon")
    return jax.shard_map(body, mesh=mesh, in_specs=in_specs, out_specs=out_specs, check_vma=False)
```

```python
from functools import partial

import jax
import jax.numpy as jnp
from jax import lax
from jax.experimental import pallas as pl
from jax.experimental.pallas import tpu as pltpu
from jax.sharding import PartitionSpec as P

SWEEPS = 4
F32 = jnp.float32
I32 = jnp.int32
SECTORS = 16
Z_PAIRS = [[4 * y + c, 4 * y + 2 + c] for y in range(4) for c in range(2)]
SIDES = [[4 * y + 2 * z + c for y in range(4) for c in range(2)] for z in range(2)]


def iota(shape, dim):
    return lax.broadcasted_iota(I32, shape, dim)


def cubic_weights(frac):
    return (
        -frac * (frac - 1.0) * (frac - 2.0) / 6.0,
        (frac + 1.0) * (frac - 1.0) * (frac - 2.0) / 2.0,
        -(frac + 1.0) * frac * (frac - 2.0) / 2.0,
        (frac + 1.0) * frac * (frac - 1.0) / 6.0,
    )


def offset_weights(frac, cells, lowest, highest):
    w = cubic_weights(frac)
    result = []
    for offset in range(-1 - highest, 3 - lowest):
        total = jnp.zeros_like(frac)
        for k in range(4):
            c = k - 1 - offset
            if lowest <= c <= highest:
                total = jnp.where(cells == float(c), w[k], total)
        result.append(total)
    return result


def pack_rows(first, second, top):
    a = jnp.where(top, first, pltpu.roll(first, 4, 0))
    b = jnp.where(top, pltpu.roll(second, 4, 0), second)
    return jnp.where(iota((8, 128), 0) < 4, a, b)


def unpack_rows(packed):
    low = iota((8, 128), 0) < 4
    turned = pltpu.roll(packed, 4, 0)
    return jnp.where(low, packed, turned), jnp.where(low, turned, packed)


def fold(x):
    lane = iota((8, 128), 1)
    low, early = lane < 80, (lane & 7) < 4
    first = jnp.where(early, x[0:8], pltpu.roll(x[8:16], 4, 1))
    second = jnp.where(early, pltpu.roll(x[16:24], 80, 1), pltpu.roll(x[16:24], 36, 1))
    return jnp.where(low, first, second)


def unfold(x):
    lane = iota((8, 128), 1)
    third = jnp.where(lane < 48, pltpu.roll(x, 48, 1), pltpu.roll(x, 92, 1))
    return jnp.concatenate([x, pltpu.roll(x, 124, 1), third], axis=0)


def pack_kernel(*refs):
    sources, out, begin, held, sems = refs[:7], refs[7], refs[8], refs[9:16], refs[16]
    loads = [pltpu.make_async_copy(s, h, sems.at[i]) for i, (s, h) in enumerate(zip(sources, held))]
    for copy in loads:
        copy.start()
    for copy in loads[1:]:
        copy.wait()
    state, shift, coefs = held[0], held[1], held[2:]
    rows = state.shape[1]
    group = iota((rows, 128), 1) // 8
    edges = jnp.zeros((rows, 128), F32)
    for i, ref in enumerate(coefs):
        for l in range(2):
            a = 2 * i + l
            edges = jnp.where(group == a, pltpu.roll(ref[l].astype(F32), 8 * a + 4, 1), edges)
    eye = iota((rows, rows), 0) == iota((rows, rows), 1)
    for l in range(2):
        line = jnp.broadcast_to(shift[l : l + 1, :].astype(F32), (rows, rows))
        moved = jnp.sum(jnp.where(eye, line, 0.0), axis=1, keepdims=True).astype(I32)
        begin[l] = jnp.broadcast_to((-moved - 7) & 2047, (rows, 128))
    loads[0].wait()
    for fl in range(8):
        out[fl] = state[fl]
    out[8] = edges


def windows(circle, begin, l, at, target, fields):
    me = lax.axis_index("lon")
    first = begin[l, at : at + 8]
    spot = (first & 127) + iota((8, 128), 1)
    index, inside = spot & 127, spot < 128
    sector = ((me ^ target) + (first >> 7) - (me & 2)) & 15
    for fl in fields:
        block = [jnp.zeros((8, 128), F32) for _ in range(3)]
        for y in range(4):
            for c in range(2):
                value = circle[2 * y + c, fl, at : at + 8]
                for k in range(3):
                    block[k] = jnp.where(sector == ((4 * y + c - k) & 15), value, block[k])
        r = [jnp.take_along_axis(v, index, axis=1) for v in block]
        yield fl, jnp.where(inside, r[0], r[1]), jnp.where(inside, r[1], r[2])


def window_kernel(target, circle, begin, out):
    rows = circle.shape[2]
    me = lax.axis_index("lon")
    core = me & 1
    slot = iota((8, 128), 1) // 16
    for at in range(0, rows, 8):
        tails = jnp.zeros((8, 128), F32)
        for l in range(2):
            for fl, head, tail in windows(circle, begin, l, at, target, range(l, 8, 2)):
                out[rows * fl + at : rows * fl + at + 8] = head
                tails = jnp.where(slot == fl, pltpu.roll(tail, 16 * fl, 1) if fl else tail, tails)
        out[8 * rows + at : 8 * rows + at + 8] = tails
    if target == 0:
        out[9 * rows : 10 * rows] = circle[me // 4 * 2 + 1 - core, 8]
    else:
        outer = ((me ^ 2) + jnp.where(core == 0, 15, 1)) & 15
        outer = circle[outer // 4 * 2 + 1 - core, 8]
        outer = jnp.where(core == 0, outer, pltpu.roll(outer, 124, 1))
        out[9 * rows : 9 * rows + 8] = fold(outer)


def zonal_kernel(keep, swapped, zc, zf, mc, mf, cp, out, ea, eb):
    rows = zc.shape[1]
    me, band = lax.axis_index("lon"), lax.axis_index("lat")
    core = me & 1
    across = 1 - ((me >> 1) & 1)
    lane = iota((rows, 128), 1)
    outer = unfold(swapped[across, 9 * rows : 9 * rows + 8])
    outer = jnp.where(core == 0, outer, pltpu.roll(outer, 4, 1))
    early = jnp.where((lane & 7) < 4, 0, 1)
    beside = jnp.where(early == core, outer, keep[9 * rows : 10 * rows])

    def both(plane):
        at = plane * rows
        return keep[at : at + rows] + swapped[across, at : at + rows]

    def extended(ref, i, l):
        a = 2 * i + l
        own = pltpu.roll(ref[l].astype(F32), 4, 1)
        side = pltpu.roll(beside, 128 - 8 * a, 1) if a else beside
        return jnp.where(lane < 4, side, own), jnp.where(lane < 4, own, side)

    ends = both(8)
    slot = lane // 8
    tails = jnp.zeros((rows, 128), F32)
    for l in range(2):
        cells, frac = extended(zc, 0, l), extended(zf, 1, l)
        near, far = [offset_weights(frac[n], cells[n], -2, 2) for n in range(2)]
        fields = range(l, 8, 2)
        heads = {fl: both(fl) for fl in fields}
        rests = {fl: pltpu.roll(ends, 128 - 16 * fl, 1) if fl else ends for fl in fields}
        total = {fl: near[0] * heads[fl] for fl in fields}
        tail = {fl: far[0] * rests[fl] for fl in fields}
        for d in range(1, 8):
            for fl in fields:
                moved = pltpu.roll(rests[fl], 128 - d, 1)
                shifted = jnp.where(lane < 128 - d, pltpu.roll(heads[fl], 128 - d, 1), moved)
                total[fl] = total[fl] + near[d] * shifted
                tail[fl] = tail[fl] + far[d] * moved
        for fl in fields:
            out[fl] = total[fl]
            end = pltpu.roll(tail[fl], 8 * fl, 1) if fl else tail[fl]
            tails = jnp.where(slot == fl, end, tails)
    for i, ref in enumerate((mc, mf, cp)):
        for l in range(2):
            a = 8 + 2 * i + l
            out[a + 1], tail = extended(ref, i + 2, l)
            tails = jnp.where(slot == a, pltpu.roll(tail, 8 * a, 1), tails)
    out[8] = tails

    even = (band & 1) == 0
    for e, top in ((ea, jnp.logical_not(even)), (eb, even)):
        take = pl.ds(pl.multiple_of(jnp.where(top, 0, rows - 8), 8), 8)
        for plane in range(9):
            e[plane] = out[plane, take]
        for i in range(3):
            e[9 + i] = pack_rows(out[9 + 2 * i, take], out[10 + 2 * i, take], top)


def source_kernel(main, ga, gb, now, fixed, scale):
    rows = main.shape[1]
    total = rows + 8
    band, bands = lax.axis_index("lat"), lax.axis_size("lat")
    even = (band & 1) == 0
    lane, row = iota((total, 128), 1), iota((total, 128), 0)
    outside = ((row < 4) & (band == 0)) | ((row >= rows + 4) & (band == bands - 1))
    tall = iota((rows + 16, 128), 0)
    beyond = ((tall < 8) & (band == 0)) | ((tall >= rows + 8) & (band == bands - 1))

    def pick(plane):
        above = jnp.where(even, gb[plane], ga[0, plane])
        below = jnp.where(even, ga[1, plane], gb[plane])
        return above, below

    def joined(ends, own):
        return jnp.concatenate([ends[0], own, ends[1]], axis=0)

    def rotated(x, lanes):
        return pltpu.roll(x, lanes % 128, 1) if lanes % 128 else x

    def prepare(cells, frac, coupling):
        weights = offset_weights(frac, cells, -1, 1)
        inverse = jnp.where(outside, 0.0, 1.0 / (1.0 + 4.0 * coupling))
        return weights, inverse, coupling * inverse

    def source_of(values, weights):
        values = [jnp.where(beyond, 0.0, v) for v in values]
        sources = [jnp.zeros((total, 128), F32) for _ in values]
        for i in range(6):
            for n, value in enumerate(values):
                moved = pltpu.roll(value, rows + 16 - (2 + i), 0)[:total]
                sources[n] = sources[n] + weights[i] * moved
        return [jnp.where(outside, 0.0, v) for v in sources]

    packs = [[unpack_rows(v) for v in pick(9 + i)] for i in range(3)]
    tails = joined(pick(8), main[8])
    edge = pltpu.roll(tails, rows + 12, 0)[:total]
    group = []
    for i in range(3):
        v = rotated(edge, 64 - 16 * i)
        v = jnp.where(lane < 16, v, pltpu.roll(v, 16, 1))
        group.append(jnp.where(lane < 32, v, pltpu.roll(v, 32, 1)))
    weights, inverse, tail_factor = prepare(*group)
    (tail,) = source_of([tails], weights)
    tail_source = tail * inverse
    phi, source, factor = [None] * 8, [None] * 8, [None] * 8
    for l in range(2):
        coefs = []
        for i in range(3):
            own = joined([v[l] for v in packs[i]], main[9 + 2 * i + l])
            coefs.append(pltpu.roll(own, rows + 12, 0)[:total])
        weights, inverse, level_factor = prepare(*coefs)
        fields = range(l, 8, 2)
        values = source_of([joined(pick(fl), main[fl]) for fl in fields], weights)
        for fl, value in zip(fields, values):
            phi[fl] = rotated(value, 8 * fl)
            source[fl] = rotated(value * inverse, 8 * fl)
            factor[fl] = rotated(level_factor, 8 * fl)
    for n, v in enumerate(phi + [tail]):
        now[n] = v
    for n, v in enumerate(source + [tail_source]):
        fixed[n] = v
    for n, v in enumerate(factor + [tail_factor]):
        scale[n] = v


def sweep_kernel(now, fixed, scale, result):
    total = now.shape[1]
    rows = total - 8
    lane = iota((total, 128), 1)
    phi, tail = [now[fl] for fl in range(8)], now[8]
    source, tail_source = [fixed[fl] for fl in range(8)], fixed[8]
    factor, tail_factor = [scale[fl] for fl in range(8)], scale[8]

    def rotated(x, lanes):
        return pltpu.roll(x, lanes % 128, 1) if lanes % 128 else x

    for sweep in range(SWEEPS):
        tail_left, tail_right = pltpu.roll(tail, 1, 1), pltpu.roll(tail, 127, 1)
        lefts = [pltpu.roll(v, 1, 1) for v in phi]
        for fl in range(8):
            tail_left = jnp.where(lane == 8 * fl, lefts[fl], tail_left)
        beside = pltpu.roll(tail, 1, 0) + pltpu.roll(tail, total - 1, 0)
        tail = tail_source + tail_factor * (beside + tail_left + tail_right)
        for fl in range(8):
            old = phi[fl]
            right = jnp.where(lane == (8 * fl - 1) % 128, tail_right, pltpu.roll(old, 127, 1))
            beside = pltpu.roll(old, 1, 0) + pltpu.roll(old, total - 1, 0) + lefts[fl] + right
            phi[fl] = source[fl] + factor[fl] * beside
            if sweep == SWEEPS - 1:
                whole = jnp.where((lane >= 8 * fl) & (lane < 8 * fl + 4), tail, phi[fl])
                whole = rotated(whole, -4 - 8 * fl)
                result[fl] = pltpu.roll(whole, total - 4, 0)[:rows]


def call(kernel, shapes, limit=32, **more):
    return pl.pallas_call(
        kernel,
        out_shape=[jax.ShapeDtypeStruct(s, d) for s, d in shapes],
        compiler_params=pltpu.CompilerParams(vmem_limit_bytes=limit << 20),
        **more,
    )


def body(state, zonal_shift, zonal_cells, zonal_fraction, merid_cells, merid_fraction, coupling):
    rows = state.shape[2]
    bands = lax.axis_size("lat")
    coefs = (zonal_cells, zonal_fraction, merid_cells, merid_fraction, coupling)
    loads = (state.reshape(8, rows, 128), zonal_shift, *coefs)
    lat_pairs = [
        [i * SECTORS + s, (i + 1) * SECTORS + s] for i in range(0, bands, 2) for s in range(SECTORS)
    ]
    lat_swaps = [p for i in range(1, bands - 1, 2) for p in ((i, i + 1), (i + 1, i))]

    hbm = pl.BlockSpec(memory_space=pltpu.HBM)
    packed, begin = call(
        pack_kernel,
        [((9, rows, 128), F32), ((2, rows, 128), I32)],
        32,
        scratch_shapes=[pltpu.VMEM(v.shape, v.dtype) for v in loads]
        + [pltpu.SemaphoreType.DMA((7,))],
        in_specs=[hbm] * 7,
    )(*[pltpu.with_memory_space_constraint(v, pltpu.HBM) for v in loads])
    circle = lax.all_gather(packed, "lon", axis_index_groups=SIDES)
    (send,) = call(partial(window_kernel, 2), [((9 * rows + 8, 128), F32)])(circle, begin)
    (keep,) = call(partial(window_kernel, 0), [((10 * rows, 128), F32)])(circle, begin)
    swapped = lax.all_gather(send, "lon", axis_index_groups=Z_PAIRS)
    main, ea, eb = call(
        zonal_kernel, [((15, rows, 128), F32), ((12, 8, 128), F32), ((12, 8, 128), F32)]
    )(keep, swapped, *coefs)
    gb = lax.ppermute(eb, "lat", lat_swaps)
    ga = lax.all_gather(ea, ("lat", "lon"), axis_index_groups=lat_pairs)
    prepared = call(source_kernel, [((9, rows + 8, 128), F32)] * 3)(main, ga, gb)
    (advanced,) = call(sweep_kernel, [((8, rows, 128), F32)])(*prepared)
    return advanced.reshape(state.shape)


def solution(mesh):
    in_specs = (
        P(None, None, "lat", "lon"),
        P(None, "lat"),
        P(None, "lat", "lon"),
        P(None, "lat", "lon"),
        P(None, "lat", "lon"),
        P(None, "lat", "lon"),
        P(None, "lat", "lon"),
    )
    out_specs = P(None, None, "lat", "lon")
    return jax.shard_map(body, mesh=mesh, in_specs=in_specs, out_specs=out_specs, check_vma=False)
```

```python
from functools import partial

import jax
import jax.numpy as jnp
from jax import lax
from jax.experimental import pallas as pl
from jax.experimental.pallas import tpu as pltpu
from jax.sharding import PartitionSpec as P

SWEEPS = 4
F32 = jnp.float32
I32 = jnp.int32
SECTORS = 16
Z_PAIRS = [[4 * y + 2 + c, 4 * y + c] for y in range(4) for c in range(2)]
SIDES = [[4 * y + 2 * z + c for y in range(4) for c in range(2)] for z in range(2)]


def iota(shape, dim):
    return lax.broadcasted_iota(I32, shape, dim)


def cubic_weights(frac):
    return (
        -frac * (frac - 1.0) * (frac - 2.0) / 6.0,
        (frac + 1.0) * (frac - 1.0) * (frac - 2.0) / 2.0,
        -(frac + 1.0) * frac * (frac - 2.0) / 2.0,
        (frac + 1.0) * frac * (frac - 1.0) / 6.0,
    )


def offset_weights(frac, cells, lowest, highest):
    w = cubic_weights(frac)
    result = []
    for offset in range(-1 - highest, 3 - lowest):
        total = jnp.zeros_like(frac)
        for k in range(4):
            c = k - 1 - offset
            if lowest <= c <= highest:
                total = jnp.where(cells == float(c), w[k], total)
        result.append(total)
    return result


def pack_rows(first, second, top):
    a = jnp.where(top, first, pltpu.roll(first, 4, 0))
    b = jnp.where(top, pltpu.roll(second, 4, 0), second)
    return jnp.where(iota((8, 128), 0) < 4, a, b)


def unpack_rows(packed):
    low = iota((8, 128), 0) < 4
    turned = pltpu.roll(packed, 4, 0)
    return jnp.where(low, packed, turned), jnp.where(low, turned, packed)


def fold(x):
    lane = iota((8, 128), 1)
    low, early = lane < 80, (lane & 7) < 4
    first = jnp.where(early, x[0:8], pltpu.roll(x[8:16], 4, 1))
    second = jnp.where(early, pltpu.roll(x[16:24], 80, 1), pltpu.roll(x[16:24], 36, 1))
    return jnp.where(low, first, second)


def unfold(x):
    lane = iota((8, 128), 1)
    third = jnp.where(lane < 48, pltpu.roll(x, 48, 1), pltpu.roll(x, 92, 1))
    return jnp.concatenate([x, pltpu.roll(x, 124, 1), third], axis=0)


def pack_kernel(*refs):
    sources, out, begin, held, sems = refs[:7], refs[7], refs[8], refs[9:16], refs[16]
    loads = [pltpu.make_async_copy(s, h, sems.at[i]) for i, (s, h) in enumerate(zip(sources, held))]
    for copy in loads:
        copy.start()
    for copy in loads[1:]:
        copy.wait()
    state, shift, coefs = held[0], held[1], held[2:]
    rows = state.shape[1]
    group = iota((rows, 128), 1) // 8
    edges = jnp.zeros((rows, 128), F32)
    for i, ref in enumerate(coefs):
        for l in range(2):
            a = 2 * i + l
            edges = jnp.where(group == a, pltpu.roll(ref[l].astype(F32), 8 * a + 4, 1), edges)
    eye = iota((rows, rows), 0) == iota((rows, rows), 1)
    for l in range(2):
        line = jnp.broadcast_to(shift[l : l + 1, :].astype(F32), (rows, rows))
        moved = jnp.sum(jnp.where(eye, line, 0.0), axis=1, keepdims=True).astype(I32)
        begin[l] = jnp.broadcast_to((-moved - 7) & 2047, (rows, 128))
    loads[0].wait()
    for fl in range(8):
        out[fl] = state[fl]
    out[8] = edges


def windows(circle, begin, l, at, target, fields):
    me = lax.axis_index("lon")
    first = begin[l, at : at + 8]
    spot = (first & 127) + iota((8, 128), 1)
    index, inside = spot & 127, spot < 128
    sector = ((me ^ target) + (first >> 7) - (me & 2)) & 15
    for fl in fields:
        block = [jnp.zeros((8, 128), F32) for _ in range(3)]
        for y in range(4):
            for c in range(2):
                value = circle[2 * y + c, fl, at : at + 8]
                for k in range(3):
                    block[k] = jnp.where(sector == ((4 * y + c - k) & 15), value, block[k])
        r = [jnp.take_along_axis(v, index, axis=1) for v in block]
        yield fl, jnp.where(inside, r[0], r[1]), jnp.where(inside, r[1], r[2])


def window_kernel(target, circle, begin, out):
    rows = circle.shape[2]
    me = lax.axis_index("lon")
    core = me & 1
    slot = iota((8, 128), 1) // 16
    for at in range(0, rows, 8):
        tails = jnp.zeros((8, 128), F32)
        for l in range(2):
            for fl, head, tail in windows(circle, begin, l, at, target, range(l, 8, 2)):
                out[rows * fl + at : rows * fl + at + 8] = head
                tails = jnp.where(slot == fl, pltpu.roll(tail, 16 * fl, 1) if fl else tail, tails)
        out[8 * rows + at : 8 * rows + at + 8] = tails
    if target == 0:
        out[9 * rows : 10 * rows] = circle[me // 4 * 2 + 1 - core, 8]
    else:
        outer = ((me ^ 2) + jnp.where(core == 0, 15, 1)) & 15
        outer = circle[outer // 4 * 2 + 1 - core, 8]
        outer = jnp.where(core == 0, outer, pltpu.roll(outer, 124, 1))
        out[9 * rows : 9 * rows + 8] = fold(outer)


def zonal_kernel(keep, swapped, zc, zf, mc, mf, cp, out, ea, eb):
    rows = zc.shape[1]
    me, band = lax.axis_index("lon"), lax.axis_index("lat")
    core = me & 1
    across = (me >> 1) & 1
    lane = iota((rows, 128), 1)
    outer = unfold(swapped[across, 9 * rows : 9 * rows + 8])
    outer = jnp.where(core == 0, outer, pltpu.roll(outer, 4, 1))
    early = jnp.where((lane & 7) < 4, 0, 1)
    beside = jnp.where(early == core, outer, keep[9 * rows : 10 * rows])

    def both(plane):
        at = plane * rows
        return keep[at : at + rows] + swapped[across, at : at + rows]

    def extended(ref, i, l):
        a = 2 * i + l
        own = pltpu.roll(ref[l].astype(F32), 4, 1)
        side = pltpu.roll(beside, 128 - 8 * a, 1) if a else beside
        return jnp.where(lane < 4, side, own), jnp.where(lane < 4, own, side)

    ends = both(8)
    slot = lane // 8
    tails = jnp.zeros((rows, 128), F32)
    for l in range(2):
        cells, frac = extended(zc, 0, l), extended(zf, 1, l)
        near, far = [offset_weights(frac[n], cells[n], -2, 2) for n in range(2)]
        fields = range(l, 8, 2)
        heads = {fl: both(fl) for fl in fields}
        rests = {fl: pltpu.roll(ends, 128 - 16 * fl, 1) if fl else ends for fl in fields}
        total = {fl: near[0] * heads[fl] for fl in fields}
        tail = {fl: far[0] * rests[fl] for fl in fields}
        for d in range(1, 8):
            for fl in fields:
                moved = pltpu.roll(rests[fl], 128 - d, 1)
                shifted = jnp.where(lane < 128 - d, pltpu.roll(heads[fl], 128 - d, 1), moved)
                total[fl] = total[fl] + near[d] * shifted
                tail[fl] = tail[fl] + far[d] * moved
        for fl in fields:
            out[fl] = total[fl]
            end = pltpu.roll(tail[fl], 8 * fl, 1) if fl else tail[fl]
            tails = jnp.where(slot == fl, end, tails)
    for i, ref in enumerate((mc, mf, cp)):
        for l in range(2):
            a = 8 + 2 * i + l
            out[a + 1], tail = extended(ref, i + 2, l)
            tails = jnp.where(slot == a, pltpu.roll(tail, 8 * a, 1), tails)
    out[8] = tails

    even = (band & 1) == 0
    for e, top in ((ea, jnp.logical_not(even)), (eb, even)):
        take = pl.ds(pl.multiple_of(jnp.where(top, 0, rows - 8), 8), 8)
        for plane in range(9):
            e[plane] = out[plane, take]
        for i in range(3):
            e[9 + i] = pack_rows(out[9 + 2 * i, take], out[10 + 2 * i, take], top)


def sweep_kernel(main, ga, gb, result, done, sems):
    rows = main.shape[1]
    total = rows + 8
    band, bands = lax.axis_index("lat"), lax.axis_size("lat")
    even = (band & 1) == 0
    lane, row = iota((total, 128), 1), iota((total, 128), 0)
    outside = ((row < 4) & (band == 0)) | ((row >= rows + 4) & (band == bands - 1))
    tall = iota((rows + 16, 128), 0)
    beyond = ((tall < 8) & (band == 0)) | ((tall >= rows + 8) & (band == bands - 1))

    def pick(plane):
        above = jnp.where(even, gb[plane], ga[0, plane])
        below = jnp.where(even, ga[1, plane], gb[plane])
        return above, below

    def joined(ends, own):
        return jnp.concatenate([ends[0], own, ends[1]], axis=0)

    def rotated(x, lanes):
        return pltpu.roll(x, lanes % 128, 1) if lanes % 128 else x

    def prepare(cells, frac, coupling):
        weights = offset_weights(frac, cells, -1, 1)
        inverse = jnp.where(outside, 0.0, 1.0 / (1.0 + 4.0 * coupling))
        return weights, inverse, coupling * inverse

    def source_of(values, weights):
        values = [jnp.where(beyond, 0.0, v) for v in values]
        sources = [jnp.zeros((total, 128), F32) for _ in values]
        for i in range(6):
            for n, value in enumerate(values):
                moved = pltpu.roll(value, rows + 16 - (2 + i), 0)[:total]
                sources[n] = sources[n] + weights[i] * moved
        return [jnp.where(outside, 0.0, v) for v in sources]

    packs = [[unpack_rows(v) for v in pick(9 + i)] for i in range(3)]
    tails = joined(pick(8), main[8])
    edge = pltpu.roll(tails, rows + 12, 0)[:total]
    group = []
    for i in range(3):
        v = rotated(edge, 64 - 16 * i)
        v = jnp.where(lane < 16, v, pltpu.roll(v, 16, 1))
        group.append(jnp.where(lane < 32, v, pltpu.roll(v, 32, 1)))
    weights, inverse, tail_factor = prepare(*group)
    (tail,) = source_of([tails], weights)
    tail_source = tail * inverse
    phi, source, factor = [None] * 8, [None] * 8, [None] * 8
    for l in range(2):
        coefs = []
        for i in range(3):
            own = joined([v[l] for v in packs[i]], main[9 + 2 * i + l])
            coefs.append(pltpu.roll(own, rows + 12, 0)[:total])
        weights, inverse, level_factor = prepare(*coefs)
        fields = range(l, 8, 2)
        values = source_of([joined(pick(fl), main[fl]) for fl in fields], weights)
        for fl, value in zip(fields, values):
            phi[fl] = rotated(value, 8 * fl)
            source[fl] = rotated(value * inverse, 8 * fl)
            factor[fl] = rotated(level_factor, 8 * fl)
    copies = []
    for sweep in range(SWEEPS):
        tail_left, tail_right = pltpu.roll(tail, 1, 1), pltpu.roll(tail, 127, 1)
        lefts = [pltpu.roll(v, 1, 1) for v in phi]
        for fl in range(8):
            tail_left = jnp.where(lane == 8 * fl, lefts[fl], tail_left)
        beside = pltpu.roll(tail, 1, 0) + pltpu.roll(tail, total - 1, 0)
        tail = tail_source + tail_factor * (beside + tail_left + tail_right)
        for fl in range(8):
            old = phi[fl]
            right = jnp.where(lane == (8 * fl - 1) % 128, tail_right, pltpu.roll(old, 127, 1))
            beside = pltpu.roll(old, 1, 0) + pltpu.roll(old, total - 1, 0) + lefts[fl] + right
            phi[fl] = source[fl] + factor[fl] * beside
            if sweep == SWEEPS - 1:
                whole = jnp.where((lane >= 8 * fl) & (lane < 8 * fl + 4), tail, phi[fl])
                whole = rotated(whole, -4 - 8 * fl)
                done[fl] = pltpu.roll(whole, total - 4, 0)[:rows]
                copies.append(pltpu.make_async_copy(done.at[fl], result.at[fl], sems.at[fl]))
                copies[-1].start()
    for copy in copies:
        copy.wait()


def call(kernel, shapes, limit=32, **more):
    return pl.pallas_call(
        kernel,
        out_shape=[jax.ShapeDtypeStruct(s, d) for s, d in shapes],
        compiler_params=pltpu.CompilerParams(vmem_limit_bytes=limit << 20),
        **more,
    )


def body(state, zonal_shift, zonal_cells, zonal_fraction, merid_cells, merid_fraction, coupling):
    rows = state.shape[2]
    bands = lax.axis_size("lat")
    coefs = (zonal_cells, zonal_fraction, merid_cells, merid_fraction, coupling)
    loads = (state.reshape(8, rows, 128), zonal_shift, *coefs)
    lat_pairs = [
        [i * SECTORS + s, (i + 1) * SECTORS + s] for i in range(0, bands, 2) for s in range(SECTORS)
    ]
    lat_swaps = [p for i in range(1, bands - 1, 2) for p in ((i, i + 1), (i + 1, i))]

    hbm = pl.BlockSpec(memory_space=pltpu.HBM)
    packed, begin = call(
        pack_kernel,
        [((9, rows, 128), F32), ((2, rows, 128), I32)],
        32,
        scratch_shapes=[pltpu.VMEM(v.shape, v.dtype) for v in loads]
        + [pltpu.SemaphoreType.DMA((7,))],
        in_specs=[hbm] * 7,
    )(*[pltpu.with_memory_space_constraint(v, pltpu.HBM) for v in loads])
    circle = lax.all_gather(packed, "lon", axis_index_groups=SIDES)
    (send,) = call(partial(window_kernel, 2), [((9 * rows + 8, 128), F32)])(circle, begin)
    (keep,) = call(partial(window_kernel, 0), [((10 * rows, 128), F32)])(circle, begin)
    swapped = lax.all_gather(send, "lon", axis_index_groups=Z_PAIRS)
    main, ea, eb = call(
        zonal_kernel, [((15, rows, 128), F32), ((12, 8, 128), F32), ((12, 8, 128), F32)]
    )(keep, swapped, *coefs)
    gb = lax.ppermute(eb, "lat", lat_swaps)
    ga = lax.all_gather(ea, ("lat", "lon"), axis_index_groups=lat_pairs)
    (advanced,) = call(
        sweep_kernel,
        [((8, rows, 128), F32)],
        scratch_shapes=[pltpu.VMEM((8, rows, 128), F32), pltpu.SemaphoreType.DMA((8,))],
        out_specs=[hbm],
    )(main, ga, gb)
    return advanced.reshape(state.shape)


def solution(mesh):
    in_specs = (
        P(None, None, "lat", "lon"),
        P(None, "lat"),
        P(None, "lat", "lon"),
        P(None, "lat", "lon"),
        P(None, "lat", "lon"),
        P(None, "lat", "lon"),
        P(None, "lat", "lon"),
    )
    out_specs = P(None, None, "lat", "lon")
    return jax.shard_map(body, mesh=mesh, in_specs=in_specs, out_specs=out_specs, check_vma=False)
```
